32 devices in a mesh: groups: 2 (over y), ctx: 16 (over z, x, core).
Axes of the slice: x: 2, y: 2, z: 4, core: 2. Of those that a mesh axis runs over, the one named last changes fastest.
Arguments:
- queries: bfloat16 [512, 5120], P(('groups', 'ctx')), parts along dimension 0, may hold values from -45 to 45
- keys: bfloat16 [49152, 1024], P(('groups', 'ctx')), parts along dimension 0, may hold values from -5 to 5
- values: bfloat16 [49152, 1024], P(('groups', 'ctx')), parts along dimension 0, may hold values from -10 to 10
- block_mask: int32 [16, 2, 192], P('groups', None, 'ctx'), parts along dimension 0, may hold values from 0 to 1, as said below
- out_weight: bfloat16 [5120, 5120], P('ctx'), may hold values from -0.078125 to 0.078125
Outputs:
- projected: bfloat16 [512, 5120], P(('groups', 'ctx')), parts along dimension 0
The draws below stay inside these ranges and needn't reach their ends.
There are 2 independent parts, one for each index of `groups`. The reference program is written for one: setup_inputs(seed, part) draws one part's arguments, and reference() takes and returns one part's arrays. A program takes and returns all parts, laid end to end along the dimension named above; an argument that names none is the same for every part. Nothing has to cross between parts.
Inputs may be any that keep to these rules, and one draw needn't show every extreme that they name: `block_mask`: for every key head and query block at least one key block is 1; the share of 1s differs between spans of 1536 positions.
All inputs are finite; a program needn't handle non-finite values.
Results may differ from the reference program's by a relative error of at most 0.0055.
Values may be sent and summed in bfloat16 or wider, within the bound.
A program may use at most 128 MiB of HBM per device.

```python
import math
import jax
import jax.numpy as jnp
from jax import lax

D = 5120
QUERY_HEADS = 40
KEY_VALUE_HEADS = 8
HEAD_SIZE = 128
MASK_BLOCK_SIZE = 128
QUERY_TOKENS = 256
KDEV = 1536
CACHED_POSITIONS = 24576


def forced_blocks(key):
    return jax.random.randint(jax.random.fold_in(key, 11), (KEY_VALUE_HEADS, QUERY_TOKENS // MASK_BLOCK_SIZE), 0, CACHED_POSITIONS // MASK_BLOCK_SIZE)


def shared_keys(key):
    base_random_key = jax.random.fold_in(key, 21)
    flattened_rows = jnp.clip(jax.random.normal(base_random_key, (CACHED_POSITIONS, KEY_VALUE_HEADS * HEAD_SIZE), jnp.float32), -5.0, 5.0)
    return flattened_rows


def draw_keys(key, part):
    flattened_rows = shared_keys(key)
    return flattened_rows.astype(jnp.bfloat16)


def draw_queries(key, part):
    query_key = jax.random.fold_in(key, 31)
    flattened_rows = jnp.clip(3.0 * jax.random.normal(query_key, (QUERY_TOKENS, D), jnp.float32), -18.0, 18.0)
    return flattened_rows.astype(jnp.bfloat16)


def draw_block_mask(key, part):
    query_block_count = QUERY_TOKENS // MASK_BLOCK_SIZE
    key_block_count = CACHED_POSITIONS // MASK_BLOCK_SIZE
    spans = CACHED_POSITIONS // KDEV
    share = jax.random.randint(jax.random.fold_in(key, 41), (spans,), 15, 56)
    share = jnp.repeat(share, KDEV // MASK_BLOCK_SIZE)
    random_rolls = jax.random.randint(jax.random.fold_in(key, 42), (KEY_VALUE_HEADS, query_block_count, key_block_count), 0, 100)
    live = random_rolls < share[None, None, :]
    forced = forced_blocks(key)
    hit = jnp.arange(key_block_count)[None, None, :] == forced[:, :, None]
    return (live | hit).astype(jnp.int32)


def level_of(stream_key, dims, pieces, smallest, largest):
    factor_of = 1.0
    for axis_at, parts in pieces:
        draws = jax.random.uniform(jax.random.fold_in(jax.random.fold_in(stream_key, 6), axis_at), (parts,), jnp.float32, smallest / len(pieces), largest / len(pieces))
        factor_of = factor_of * jnp.repeat(jnp.exp(draws), dims[axis_at] // parts).reshape((-1,) + (1,) * (len(dims) - 1 - axis_at))
    return factor_of


def normal_values(rng, extent, spread, limit, split=(), held_as=jnp.bfloat16):
    entries = spread * jax.random.normal(rng, extent, jnp.float32)
    if split:
        entries = entries * level_of(rng, extent, split, -0.22, 0.18)
    return jnp.clip(entries, -limit, limit).astype(held_as)


def setup_inputs(seed: int = 0, part: int = 0) -> dict:
    streams_of = jax.random.split(jax.random.key(seed), 6)
    part_splits = jax.random.split(jax.random.fold_in(streams_of[5], part), 6)
    return {
        "queries": draw_queries(jax.random.fold_in(jax.random.fold_in(streams_of[5], part), 71), part),
        "keys": draw_keys(jax.random.fold_in(jax.random.fold_in(streams_of[5], part), 71), part),
        "values": normal_values(part_splits[2], (CACHED_POSITIONS, KEY_VALUE_HEADS * HEAD_SIZE), 2.0, 10.0, ((0, 16),)),
        "block_mask": draw_block_mask(jax.random.fold_in(jax.random.fold_in(streams_of[5], part), 71), part),
        "out_weight": normal_values(streams_of[4], (D, D), D ** -0.5, 0.078125, ((0, 16),)),
    }


NEG = -1e+30

def reference(queries, keys, values, block_mask, out_weight):
    query_group = QUERY_HEADS // KEY_VALUE_HEADS
    scale = 1.0 / math.sqrt(HEAD_SIZE)
    q3 = queries.reshape(QUERY_TOKENS, QUERY_HEADS, HEAD_SIZE)
    key_tensor = keys.reshape(CACHED_POSITIONS, KEY_VALUE_HEADS, HEAD_SIZE)
    value_tensor = values.reshape(CACHED_POSITIONS, KEY_VALUE_HEADS, HEAD_SIZE)

    def one_head(head):
        kv_head = head // query_group
        q_h = lax.dynamic_index_in_dim(q3, head, 1, keepdims=False)
        k_h = lax.dynamic_index_in_dim(key_tensor, kv_head, 1, keepdims=False)
        v_h = lax.dynamic_index_in_dim(value_tensor, kv_head, 1, keepdims=False)
        scores = jnp.dot(q_h, k_h.T, preferred_element_type=jnp.float32) * scale
        blocks = lax.dynamic_index_in_dim(block_mask, kv_head, 0, keepdims=False)
        live = jnp.repeat(jnp.repeat(blocks > 0, MASK_BLOCK_SIZE, axis=0), MASK_BLOCK_SIZE, axis=1)
        top = lax.optimization_barrier(jnp.max(jnp.where(live, scores, NEG), axis=1, keepdims=True))
        probs = jnp.where(live, jnp.exp(scores - top), 0.0).astype(jnp.bfloat16)
        denom = lax.optimization_barrier(jnp.sum(probs.astype(jnp.float32), axis=1, keepdims=True))
        numer = jnp.dot(probs, v_h, preferred_element_type=jnp.float32)
        return numer / denom
    attn = lax.map(one_head, jnp.arange(QUERY_HEADS, dtype=jnp.int32))
    attn = jnp.transpose(attn, (1, 0, 2)).reshape(QUERY_TOKENS, D).astype(jnp.bfloat16)
    return jnp.dot(attn, out_weight, preferred_element_type=jnp.float32).astype(jnp.bfloat16)
```

```python
import functools
import math

import jax
import jax.numpy as jnp
from jax import lax
from jax.experimental import pallas as pl
from jax.experimental.pallas import tpu as pltpu
from jax.sharding import PartitionSpec as P

HEAD_SIZE = 128
NEG = -1e30
LOG2E = math.log2(math.e)
MESH = pl.DeviceIdType.MESH


def attend_kernel(mask_ref, q_ref, k_ref, v_ref, numer_ref, top_ref, total_ref, live_ref, score_ref):
    head = pl.program_id(0)
    query_blocks, key_blocks = mask_ref.shape[1:]
    key_block = k_ref.shape[0] // key_blocks
    query_block = q_ref.shape[0] // query_blocks
    group = q_ref.shape[1] // HEAD_SIZE
    factor = LOG2E / math.sqrt(HEAD_SIZE)
    for at in range(query_blocks):
        rows = pl.ds(at * query_block, query_block)
        count = jnp.int32(0)
        for block in range(key_blocks):
            live_ref[count] = block
            count = count + (mask_ref[head, at, block] > 0).astype(jnp.int32)
        live_ref[count] = 0
        stacked = jnp.concatenate(
            [q_ref[rows, g * HEAD_SIZE : (g + 1) * HEAD_SIZE] for g in range(group)], axis=0
        )
        lanes = stacked.shape[0]
        pairs = (count + 1) // 2

        def block_of(ref, which):
            start = pl.multiple_of(live_ref[which] * key_block, key_block)
            return ref[pl.ds(start, key_block), :]

        def score_step(pair, top):
            both = jnp.concatenate([block_of(k_ref, 2 * pair), block_of(k_ref, 2 * pair + 1)], axis=0)
            scores = lax.dot_general(
                both, stacked, (((1,), (1,)), ((), ())), preferred_element_type=jnp.float32
            ) * factor
            score_ref[pair] = scores
            half = jnp.max(scores[:key_block].reshape(key_block // 8, 8, lanes), axis=0)
            other = jnp.max(scores[key_block:].reshape(key_block // 8, 8, lanes), axis=0)
            other = jnp.where(2 * pair + 1 < count, other, NEG)
            return jnp.maximum(top, jnp.maximum(half, other))

        top = lax.fori_loop(0, pairs, score_step, jnp.full((8, lanes), NEG, jnp.float32))
        top = jnp.max(top, axis=0, keepdims=True)

        def sum_step(pair, carry):
            numer, total = carry
            probs = jnp.exp2(score_ref[pair] - top)
            upper = jnp.where(2 * pair + 1 < count, probs[key_block:], 0.0)
            probs = jnp.concatenate([probs[:key_block], upper], axis=0).astype(jnp.bfloat16)
            total = total + jnp.sum(
                probs.astype(jnp.float32).reshape(2 * key_block // 8, 8, lanes), axis=0
            )
            both = jnp.concatenate([block_of(v_ref, 2 * pair), block_of(v_ref, 2 * pair + 1)], axis=0)
            numer = numer + lax.dot_general(
                both, probs, (((0,), (0,)), ((), ())), preferred_element_type=jnp.float32
            )
            return numer, total

        numer, total = lax.fori_loop(
            0,
            pairs,
            sum_step,
            (jnp.zeros((HEAD_SIZE, lanes), jnp.float32), jnp.zeros((8, lanes), jnp.float32)),
        )
        top_ref[0, at : at + 1, :] = top
        total_ref[0, at : at + 1, :] = jnp.sum(total, axis=0, keepdims=True)
        for g in range(group):
            columns = slice(g * query_block, (g + 1) * query_block)
            numer_ref[rows, g * HEAD_SIZE : (g + 1) * HEAD_SIZE] = numer[:, columns].T.astype(
                numer_ref.dtype
            )


def attend(whole, keys, values, block_mask, numer_type):
    qtok, width = whole.shape
    kdev = keys.shape[0]
    heads_kv, query_blocks, key_blocks = block_mask.shape
    columns = width // heads_kv
    lanes = columns // HEAD_SIZE * (qtok // query_blocks)
    stat = jax.ShapeDtypeStruct((heads_kv, query_blocks, lanes), jnp.float32)
    stat_spec = pl.BlockSpec((1, query_blocks, lanes), lambda h: (h, 0, 0))
    return pl.pallas_call(
        attend_kernel,
        grid=(heads_kv,),
        out_shape=(jax.ShapeDtypeStruct((qtok, width), numer_type), stat, stat),
        in_specs=[
            pl.BlockSpec(memory_space=pltpu.SMEM),
            pl.BlockSpec((qtok, columns), lambda h: (0, h)),
            pl.BlockSpec((kdev, HEAD_SIZE), lambda h: (0, h)),
            pl.BlockSpec((kdev, HEAD_SIZE), lambda h: (0, h)),
        ],
        out_specs=(pl.BlockSpec((qtok, columns), lambda h: (0, h)), stat_spec, stat_spec),
        scratch_shapes=[
            pltpu.SMEM((key_blocks + 2,), jnp.int32),
            pltpu.VMEM(((key_blocks + 1) // 2, 2 * kdev // key_blocks, lanes), jnp.float32),
        ],
        compiler_params=pltpu.CompilerParams(vmem_limit_bytes=40 * 2**20),
        name="attend",
    )(block_mask, whole, keys, values)


def by_token(stat, qtok):
    heads_kv, query_blocks, _ = stat.shape
    stat = stat.reshape(heads_kv, query_blocks, -1, qtok // query_blocks)
    return stat.transpose(1, 3, 0, 2).reshape(qtok, -1)


def shards_any(queries, keys, values, block_mask, out_weight):
    whole = lax.all_gather(queries, "ctx", axis=0, tiled=True)
    qtok, width = whole.shape
    numer, top, total = attend(whole, keys, values, block_mask, jnp.float32)
    rescale = by_token(jnp.exp2(top - lax.pmax(top, "ctx")), qtok)
    denom = by_token(total, qtok) * rescale
    numer = (numer.reshape(qtok, -1, HEAD_SIZE) * rescale[:, :, None]).reshape(qtok, width)
    num_rows = lax.psum_scatter(numer, "ctx", scatter_dimension=0, tiled=True)
    den_rows = lax.psum_scatter(denom, "ctx", scatter_dimension=0, tiled=True)
    own_rows = num_rows.shape[0]
    attn_rows = (num_rows.reshape(own_rows, -1, HEAD_SIZE) / den_rows[:, :, None]).reshape(
        own_rows, width
    )
    attn_cols = lax.all_to_all(
        attn_rows.astype(jnp.bfloat16), "ctx", split_axis=1, concat_axis=0, tiled=True
    )
    summed = lax.psum_scatter(
        jnp.dot(attn_cols, out_weight, preferred_element_type=jnp.float32),
        "ctx",
        scatter_dimension=0,
        tiled=True,
    )
    return summed.astype(jnp.bfloat16)


def solution(mesh):
    return jax.shard_map(
        shards_any,
        mesh=mesh,
        in_specs=(
            P(("groups", "ctx"), None),
            P(("groups", "ctx"), None),
            P(("groups", "ctx"), None),
            P("groups", None, "ctx"),
            P("ctx", None),
        ),
        out_specs=P(("groups", "ctx"), None),
        check_vma=False,
    )
```

```python
import functools
import math

import jax
import jax.numpy as jnp
from jax import lax
from jax.experimental import pallas as pl
from jax.experimental.pallas import tpu as pltpu
from jax.sharding import PartitionSpec as P

HEAD_SIZE = 128
NEG = -1e30
LOG2E = math.log2(math.e)
MESH = pl.DeviceIdType.MESH


def attend_kernel(mask_ref, q_ref, k_ref, v_ref, numer_ref, top_ref, total_ref, live_ref, score_ref):
    head = pl.program_id(0)
    query_blocks, key_blocks = mask_ref.shape[1:]
    key_block = k_ref.shape[0] // key_blocks
    query_block = q_ref.shape[0] // query_blocks
    group = q_ref.shape[1] // HEAD_SIZE
    factor = LOG2E / math.sqrt(HEAD_SIZE)
    for at in range(query_blocks):
        rows = pl.ds(at * query_block, query_block)
        count = jnp.int32(0)
        for block in range(key_blocks):
            live_ref[count] = block
            count = count + (mask_ref[head, at, block] > 0).astype(jnp.int32)
        live_ref[count] = 0
        stacked = jnp.concatenate(
            [q_ref[rows, g * HEAD_SIZE : (g + 1) * HEAD_SIZE] for g in range(group)], axis=0
        )
        lanes = stacked.shape[0]
        pairs = (count + 1) // 2

        def block_of(ref, which):
            start = pl.multiple_of(live_ref[which] * key_block, key_block)
            return ref[pl.ds(start, key_block), :]

        def score_step(pair, top):
            both = jnp.concatenate([block_of(k_ref, 2 * pair), block_of(k_ref, 2 * pair + 1)], axis=0)
            scores = lax.dot_general(
                both, stacked, (((1,), (1,)), ((), ())), preferred_element_type=jnp.float32
            ) * factor
            score_ref[pair] = scores
            half = jnp.max(scores[:key_block].reshape(key_block // 8, 8, lanes), axis=0)
            other = jnp.max(scores[key_block:].reshape(key_block // 8, 8, lanes), axis=0)
            other = jnp.where(2 * pair + 1 < count, other, NEG)
            return jnp.maximum(top, jnp.maximum(half, other))

        top = lax.fori_loop(0, pairs, score_step, jnp.full((8, lanes), NEG, jnp.float32))
        top = jnp.max(top, axis=0, keepdims=True)

        def sum_step(pair, carry):
            numer, total = carry
            probs = jnp.exp2(score_ref[pair] - top)
            upper = jnp.where(2 * pair + 1 < count, probs[key_block:], 0.0)
            probs = jnp.concatenate([probs[:key_block], upper], axis=0).astype(jnp.bfloat16)
            total = total + jnp.sum(
                probs.astype(jnp.float32).reshape(2 * key_block // 8, 8, lanes), axis=0
            )
            both = jnp.concatenate([block_of(v_ref, 2 * pair), block_of(v_ref, 2 * pair + 1)], axis=0)
            numer = numer + lax.dot_general(
                both, probs, (((0,), (0,)), ((), ())), preferred_element_type=jnp.float32
            )
            return numer, total

        numer, total = lax.fori_loop(
            0,
            pairs,
            sum_step,
            (jnp.zeros((HEAD_SIZE, lanes), jnp.float32), jnp.zeros((8, lanes), jnp.float32)),
        )
        top_ref[0, at : at + 1, :] = top
        total_ref[0, at : at + 1, :] = jnp.sum(total, axis=0, keepdims=True)
        for g in range(group):
            columns = slice(g * query_block, (g + 1) * query_block)
            numer_ref[rows, g * HEAD_SIZE : (g + 1) * HEAD_SIZE] = numer[:, columns].T.astype(
                numer_ref.dtype
            )


def attend(whole, keys, values, block_mask, numer_type):
    qtok, width = whole.shape
    kdev = keys.shape[0]
    heads_kv, query_blocks, key_blocks = block_mask.shape
    columns = width // heads_kv
    lanes = columns // HEAD_SIZE * (qtok // query_blocks)
    stat = jax.ShapeDtypeStruct((heads_kv, query_blocks, lanes), jnp.float32)
    stat_spec = pl.BlockSpec((1, query_blocks, lanes), lambda h: (h, 0, 0))
    return pl.pallas_call(
        attend_kernel,
        grid=(heads_kv,),
        out_shape=(jax.ShapeDtypeStruct((qtok, width), numer_type), stat, stat),
        in_specs=[
            pl.BlockSpec(memory_space=pltpu.SMEM),
            pl.BlockSpec((qtok, columns), lambda h: (0, h)),
            pl.BlockSpec((kdev, HEAD_SIZE), lambda h: (0, h)),
            pl.BlockSpec((kdev, HEAD_SIZE), lambda h: (0, h)),
        ],
        out_specs=(pl.BlockSpec((qtok, columns), lambda h: (0, h)), stat_spec, stat_spec),
        scratch_shapes=[
            pltpu.SMEM((key_blocks + 2,), jnp.int32),
            pltpu.VMEM(((key_blocks + 1) // 2, 2 * kdev // key_blocks, lanes), jnp.float32),
        ],
        compiler_params=pltpu.CompilerParams(vmem_limit_bytes=40 * 2**20),
        name="attend",
    )(block_mask, whole, keys, values)


def by_token(stat, qtok):
    heads_kv, query_blocks, _ = stat.shape
    stat = stat.reshape(heads_kv, query_blocks, -1, qtok // query_blocks)
    return stat.transpose(1, 3, 0, 2).reshape(qtok, -1)


def shards_any(queries, keys, values, block_mask, out_weight):
    whole = lax.all_gather(queries, "ctx", axis=0, tiled=True)
    qtok, width = whole.shape
    numer, top, total = attend(whole, keys, values, block_mask, jnp.float32)
    rescale = by_token(jnp.exp2(top - lax.pmax(top, "ctx")), qtok)
    denom = by_token(total, qtok) * rescale
    numer = (numer.reshape(qtok, -1, HEAD_SIZE) * rescale[:, :, None]).reshape(qtok, width)
    num_rows = lax.psum_scatter(numer, "ctx", scatter_dimension=0, tiled=True)
    den_rows = lax.psum_scatter(denom, "ctx", scatter_dimension=0, tiled=True)
    own_rows = num_rows.shape[0]
    attn_rows = (num_rows.reshape(own_rows, -1, HEAD_SIZE) / den_rows[:, :, None]).reshape(
        own_rows, width
    )
    attn_cols = lax.all_to_all(
        attn_rows.astype(jnp.bfloat16), "ctx", split_axis=1, concat_axis=0, tiled=True
    )
    summed = lax.psum_scatter(
        jnp.dot(attn_cols, out_weight, preferred_element_type=jnp.float32),
        "ctx",
        scatter_dimension=0,
        tiled=True,
    )
    return summed.astype(jnp.bfloat16)


CORES, ROW = 2, 2


def place(n):
    me = lax.axis_index("ctx")
    core = lax.rem(me, CORES)
    x = lax.rem(me // CORES, ROW)
    plane = me // (CORES * ROW)
    return me, plane, x, core


def index_of(plane, x, core):
    return (plane * ROW + x) * CORES + core


def greet(devices):
    barrier = pltpu.get_barrier_semaphore()
    for device in devices:
        pl.semaphore_signal(barrier, inc=1, device_id={"ctx": device}, device_id_type=MESH)
    pl.semaphore_wait(barrier, len(devices))


def remote(src, dst, send, recv, device):
    return pltpu.make_async_remote_copy(
        src_ref=src,
        dst_ref=dst,
        send_sem=send,
        recv_sem=recv,
        device_id={"ctx": device},
        device_id_type=MESH,
    )


def gather_kernel(n, own_ref, whole_ref, own_sem, send_sem, recv_sem):
    me, plane, x, core = place(n)
    planes = n // (CORES * ROW)
    beside, sibling = 1 - x, 1 - core
    across = [lax.rem(plane + step, planes) for step in range(1, planes)]
    greet(
        [index_of(p, x, core) for p in across]
        + [index_of(plane, beside, core), index_of(plane, x, sibling)]
    )
    own = pltpu.make_async_copy(own_ref, whole_ref.at[me], own_sem)
    own.start()
    sends = []

    def send(src, block, slot, device):
        copy = remote(src, whole_ref.at[block], send_sem.at[slot], recv_sem.at[block], device)
        copy.start()
        sends.append(copy)

    def arrived(block, device):
        remote(own_ref, whole_ref.at[block], send_sem.at[0], recv_sem.at[block], device).wait_recv()

    slot = 0
    for p in across:
        send(own_ref, me, slot, index_of(p, x, core))
        slot += 1
    send(own_ref, me, slot, index_of(plane, beside, core))
    send(own_ref, me, slot + 1, index_of(plane, x, sibling))
    slot += 2
    for step in range(planes):
        if step:
            block = index_of(lax.rem(plane + planes - step, planes), x, core)
            arrived(block, me)
            send(whole_ref.at[block], block, slot, index_of(plane, beside, core))
            send(whole_ref.at[block], block, slot + 1, index_of(plane, x, sibling))
            slot += 2
    for step in range(planes):
        block = index_of(lax.rem(plane + planes - step, planes), beside, core)
        arrived(block, me)
        send(whole_ref.at[block], block, slot, index_of(plane, x, sibling))
        slot += 1
    for step in range(planes):
        for side in (x, beside):
            arrived(index_of(lax.rem(plane + planes - step, planes), side, sibling), me)
    for copy in sends:
        copy.wait_send()
    own.wait()


def gather_rows(queries, n):
    rows, width = queries.shape
    whole = pl.pallas_call(
        functools.partial(gather_kernel, n),
        out_shape=jax.ShapeDtypeStruct((n, rows, width), queries.dtype),
        in_specs=[pl.BlockSpec(memory_space=pltpu.VMEM)],
        out_specs=pl.BlockSpec(memory_space=pltpu.VMEM),
        scratch_shapes=[
            pltpu.SemaphoreType.DMA,
            pltpu.SemaphoreType.DMA((n,)),
            pltpu.SemaphoreType.DMA((n,)),
        ],
        compiler_params=pltpu.CompilerParams(collective_id=0, has_side_effects=True),
        name="gather_rows",
    )(queries)
    return whole.reshape(n * rows, width)


def reduce_rows(place_of, parts, merge, finish):
    plane, x, core, planes = place_of
    beside, sibling = 1 - x, 1 - core
    order = [lax.rem(plane + step, planes) for step in range(1, planes)] + [plane]

    def core_copy(part, p):
        src, got, _, _, _, _, sem = part
        return remote(
            src.at[p, :, sibling], got.at[p], sem.at[0, p], sem.at[1, p], index_of(plane, x, sibling)
        )

    def beside_copy(part, p):
        _, _, held, got, _, _, sem = part
        return remote(
            held.at[p, beside], got.at[p], sem.at[2, p], sem.at[3, p], index_of(plane, beside, core)
        )

    def plane_copy(part, p, slot):
        _, _, _, _, summed, got, sem = part
        return remote(summed.at[p], got.at[slot], sem.at[4, p], sem.at[5, slot], index_of(p, x, core))

    for p in order:
        for part in parts:
            core_copy(part, p).start()

    def turn(step):
        return lax.rem(plane + 1 + step, planes)

    def from_core(step, _):
        p = turn(step)
        for part in parts:
            core_copy(part, p).wait_recv()
        for side in range(ROW):
            merge(
                [part[0].at[p, side, core] for part in parts],
                [part[1].at[p, side] for part in parts],
                [part[2].at[p, side] for part in parts],
            )
        for part in parts:
            beside_copy(part, p).start()
        return 0

    lax.fori_loop(0, planes, from_core, 0)

    def from_beside(step, _):
        p = turn(step)
        for part in parts:
            beside_copy(part, p).wait_recv()
        merge(
            [part[2].at[p, x] for part in parts],
            [part[3].at[p] for part in parts],
            [part[4].at[p] for part in parts],
        )

        @pl.when(step < planes - 1)
        def _():
            for part in parts:
                plane_copy(part, p, plane).start()

        return 0

    lax.fori_loop(0, planes, from_beside, 0)
    for p in order[:-1]:
        for part in parts:
            plane_copy(part, p, p).wait_recv()
    finish(
        [[part[4].at[plane] for part in parts]]
        + [[part[5].at[p] for part in parts] for p in order[:-1]]
    )
    for p in order:
        for part in parts:
            core_copy(part, p).wait_send()
            beside_copy(part, p).wait_send()
    for p in order[:-1]:
        for part in parts:
            plane_copy(part, p, plane).wait_send()


def reduce_scratch(planes, rows, width, dtype):
    return [
        pltpu.VMEM((planes, ROW, rows, width), dtype),
        pltpu.VMEM((planes, ROW, rows, width), dtype),
        pltpu.VMEM((planes, rows, width), dtype),
        pltpu.VMEM((planes, rows, width), dtype),
        pltpu.VMEM((planes, rows, width), dtype),
        pltpu.SemaphoreType.DMA((6, planes)),
    ]


STATS = 128


def weigh(stats):
    half = STATS // 2
    tops = [stat[:, :half] for stat in stats]
    top = functools.reduce(jnp.maximum, tops)
    factors = [jnp.exp2(one - top) for one in tops]
    total = sum(stat[:, half:] * factor for stat, factor in zip(stats, factors))
    return top, factors, total


def combine_kernel(n, numer_ref, stat_ref, cols_ref, *scratch):
    numer_scratch, stat_scratch = scratch[:6], scratch[6:12]
    piece_ref, swap_send, swap_recv, own_sem = scratch[12:]
    me, plane, x, core = place(n)
    planes = n // (CORES * ROW)
    width = numer_ref.shape[-1]
    heads = width // HEAD_SIZE
    others = [lax.rem(me + step, n) for step in range(1, n)]
    greet(others)

    def merge(one, two, out):
        top, factors, total = weigh([one[1][...], two[1][...]])
        out[1][...] = jnp.concatenate([top, total], axis=1)
        for head in range(heads):
            at = slice(head * HEAD_SIZE, (head + 1) * HEAD_SIZE)
            out[0][:, at] = (
                one[0][:, at].astype(jnp.float32) * factors[0][:, head : head + 1]
                + two[0][:, at].astype(jnp.float32) * factors[1][:, head : head + 1]
            ).astype(out[0].dtype)

    def finish(sources):
        _, factors, total = weigh([source[1][...] for source in sources])
        out = []
        for head in range(heads):
            at = slice(head * HEAD_SIZE, (head + 1) * HEAD_SIZE)
            numer = sum(
                source[0][:, at].astype(jnp.float32) * factor[:, head : head + 1]
                for source, factor in zip(sources, factors)
            )
            out.append((numer / total[:, head : head + 1]).astype(jnp.bfloat16))
        attn = jnp.concatenate(out, axis=1)
        share = width // n
        for device in range(n):
            piece_ref[device] = attn[:, device * share : (device + 1) * share]

    reduce_rows(
        (plane, x, core, planes),
        [(numer_ref, *numer_scratch), (stat_ref, *stat_scratch)],
        merge,
        finish,
    )

    def swap(device, slot):
        return remote(
            piece_ref.at[device], cols_ref.at[slot], swap_send.at[device], swap_recv.at[slot], device
        )

    own = pltpu.make_async_copy(piece_ref.at[me], cols_ref.at[me], own_sem)
    own.start()
    for device in others:
        swap(device, me).start()
    own.wait()
    for device in others:
        swap(device, device).wait_recv()
    for device in others:
        swap(device, me).wait_send()


def combine(numer, stats, n):
    qtok, width = numer.shape
    planes, rows = n // (CORES * ROW), qtok // n
    cols = pl.pallas_call(
        functools.partial(combine_kernel, n),
        out_shape=jax.ShapeDtypeStruct((n, rows, width // n), jnp.bfloat16),
        in_specs=[pl.BlockSpec(memory_space=pltpu.VMEM)] * 2,
        out_specs=pl.BlockSpec(memory_space=pltpu.VMEM),
        scratch_shapes=reduce_scratch(planes, rows, width, jnp.bfloat16)
        + reduce_scratch(planes, rows, STATS, jnp.float32)
        + [
            pltpu.VMEM((n, rows, width // n), jnp.bfloat16),
            pltpu.SemaphoreType.DMA((n,)),
            pltpu.SemaphoreType.DMA((n,)),
            pltpu.SemaphoreType.DMA,
        ],
        compiler_params=pltpu.CompilerParams(
            collective_id=1, has_side_effects=True, vmem_limit_bytes=40 * 2**20
        ),
        name="combine",
    )(
        numer.reshape(planes, ROW, CORES, rows, width),
        stats.reshape(planes, ROW, CORES, rows, STATS),
    )
    return cols.reshape(qtok, width // n)


TILE = 512


def project_kernel(n, cols_ref, weight_ref, out_ref, part_ref, *scratch):
    _, plane, x, core = place(n)
    planes = n // (CORES * ROW)
    rows, width = out_ref.shape
    greet(
        [index_of(lax.rem(plane + step, planes), x, core) for step in range(1, planes)]
        + [index_of(plane, 1 - x, core), index_of(plane, x, 1 - core)]
    )

    def tile_step(tile, _):
        at = pl.ds(pl.multiple_of(tile * TILE, TILE), TILE)
        product = jnp.dot(cols_ref[...], weight_ref[:, at], preferred_element_type=jnp.float32)
        part_ref[:, :, :, :, at] = product.astype(part_ref.dtype).reshape(
            planes, ROW, CORES, rows, TILE
        )
        return 0

    lax.fori_loop(0, width // TILE, tile_step, 0)

    def merge(one, two, out):
        out[0][...] = (one[0][...].astype(jnp.float32) + two[0][...].astype(jnp.float32)).astype(
            out[0].dtype
        )

    def finish(sources):
        out_ref[...] = sum(source[0][...].astype(jnp.float32) for source in sources).astype(
            out_ref.dtype
        )

    reduce_rows((plane, x, core, planes), [(part_ref, *scratch)], merge, finish)


def project(cols, weight, n):
    qtok = cols.shape[0]
    width = weight.shape[1]
    planes, rows = n // (CORES * ROW), qtok // n
    return pl.pallas_call(
        functools.partial(project_kernel, n),
        out_shape=jax.ShapeDtypeStruct((rows, width), jnp.bfloat16),
        in_specs=[pl.BlockSpec(memory_space=pltpu.VMEM)] * 2,
        out_specs=pl.BlockSpec(memory_space=pltpu.VMEM),
        scratch_shapes=[pltpu.VMEM((planes, ROW, CORES, rows, width), jnp.bfloat16)]
        + reduce_scratch(planes, rows, width, jnp.bfloat16),
        compiler_params=pltpu.CompilerParams(
            collective_id=2, has_side_effects=True, vmem_limit_bytes=40 * 2**20
        ),
        name="project",
    )(cols, weight)


def shards_near(n, queries, keys, values, block_mask, out_weight):
    whole = gather_rows(queries, n)
    qtok = whole.shape[0]
    numer, top, total = attend(whole, keys, values, block_mask, jnp.bfloat16)
    top, total = by_token(top, qtok), by_token(total, qtok)
    room = ((0, 0), (0, STATS // 2 - top.shape[1]))
    stats = jnp.concatenate([jnp.pad(top, room), jnp.pad(total, room)], axis=1)
    cols = combine(numer, stats, n)
    return project(cols, out_weight, n)


def solution(mesh):
    n = mesh.shape["ctx"]

    def shards(queries, *rest):
        fits = n % (CORES * ROW) == 0 and queries.shape[0] % 16 == 0
        if fits and queries.shape[1] // HEAD_SIZE <= STATS // 2:
            return shards_near(n, queries, *rest)
        return shards_any(queries, *rest)

    return jax.shard_map(
        shards,
        mesh=mesh,
        in_specs=(
            P(("groups", "ctx"), None),
            P(("groups", "ctx"), None),
            P(("groups", "ctx"), None),
            P("groups", None, "ctx"),
            P("ctx", None),
        ),
        out_specs=P(("groups", "ctx"), None),
        check_vma=False,
    )
```

```python
import functools
import math

import jax
import jax.numpy as jnp
from jax import lax
from jax.experimental import pallas as pl
from jax.experimental.pallas import tpu as pltpu
from jax.sharding import PartitionSpec as P

HEAD_SIZE = 128
NEG = -1e30
LOG2E = math.log2(math.e)
MESH = pl.DeviceIdType.MESH
CORES, ROW = 2, 2


def attend_kernel(rows_each, mask_ref, q_ref, k_ref, v_ref, *refs):
    *numer_refs, top_ref, total_ref, live_ref, score_ref = refs
    head = pl.program_id(0)
    query_blocks, key_blocks = mask_ref.shape[1:]
    key_block = k_ref.shape[0] // key_blocks
    query_block = q_ref.shape[0] // query_blocks
    group = q_ref.shape[1] // HEAD_SIZE
    factor = LOG2E / math.sqrt(HEAD_SIZE)
    for at in range(query_blocks):
        rows = pl.ds(at * query_block, query_block)
        count = jnp.int32(0)
        for block in range(key_blocks):
            live_ref[count] = block
            count = count + (mask_ref[head, at, block] > 0).astype(jnp.int32)
        live_ref[count] = 0
        stacked = jnp.concatenate(
            [q_ref[rows, g * HEAD_SIZE : (g + 1) * HEAD_SIZE] for g in range(group)], axis=0
        )
        lanes = stacked.shape[0]
        pairs = (count + 1) // 2

        def block_of(ref, which):
            start = pl.multiple_of(live_ref[which] * key_block, key_block)
            return ref[pl.ds(start, key_block), :]

        def score_step(pair, top):
            both = jnp.concatenate([block_of(k_ref, 2 * pair), block_of(k_ref, 2 * pair + 1)], axis=0)
            scores = lax.dot_general(
                both, stacked, (((1,), (1,)), ((), ())), preferred_element_type=jnp.float32
            ) * factor
            score_ref[pair] = scores
            half = jnp.max(scores[:key_block].reshape(key_block // 8, 8, lanes), axis=0)
            other = jnp.max(scores[key_block:].reshape(key_block // 8, 8, lanes), axis=0)
            other = jnp.where(2 * pair + 1 < count, other, NEG)
            return jnp.maximum(top, jnp.maximum(half, other))

        top = lax.fori_loop(0, pairs, score_step, jnp.full((8, lanes), NEG, jnp.float32))
        top = jnp.max(top, axis=0, keepdims=True)

        def sum_step(pair, carry):
            numer, total = carry
            probs = jnp.exp2(score_ref[pair] - top)
            upper = jnp.where(2 * pair + 1 < count, probs[key_block:], 0.0)
            probs = jnp.concatenate([probs[:key_block], upper], axis=0).astype(jnp.bfloat16)
            total = total + jnp.sum(
                probs.astype(jnp.float32).reshape(2 * key_block // 8, 8, lanes), axis=0
            )
            both = jnp.concatenate([block_of(v_ref, 2 * pair), block_of(v_ref, 2 * pair + 1)], axis=0)
            numer = numer + lax.dot_general(
                both, probs, (((0,), (0,)), ((), ())), preferred_element_type=jnp.float32
            )
            return numer, total

        numer, total = lax.fori_loop(
            0,
            pairs,
            sum_step,
            (jnp.zeros((HEAD_SIZE, lanes), jnp.float32), jnp.zeros((8, lanes), jnp.float32)),
        )
        top_ref[0, at : at + 1, :] = top
        total_ref[0, at : at + 1, :] = jnp.sum(total, axis=0, keepdims=True)
        for g in range(group):
            columns = slice(g * query_block, (g + 1) * query_block)
            out_columns = slice(g * HEAD_SIZE, (g + 1) * HEAD_SIZE)
            tokens = numer[:, columns].T
            if not rows_each:
                numer_refs[0][rows, out_columns] = tokens
                continue
            tokens = tokens.reshape(-1, CORES, rows_each, HEAD_SIZE)
            first = lax.rem(lax.axis_index("ctx"), CORES) == 0
            half = pl.ds(at * query_block // CORES, query_block // CORES)
            kept = jnp.where(first, tokens[:, 0], tokens[:, 1]).reshape(-1, HEAD_SIZE)
            sent = jnp.where(first, tokens[:, 1], tokens[:, 0]).reshape(-1, HEAD_SIZE)
            numer_refs[0][half, out_columns] = kept
            numer_refs[1][half, out_columns] = sent.astype(jnp.bfloat16)


def attend(whole, keys, values, block_mask, rows_each):
    qtok, width = whole.shape
    kdev = keys.shape[0]
    heads_kv, query_blocks, key_blocks = block_mask.shape
    columns = width // heads_kv
    lanes = columns // HEAD_SIZE * (qtok // query_blocks)
    stat = jax.ShapeDtypeStruct((heads_kv, query_blocks, lanes), jnp.float32)
    stat_spec = pl.BlockSpec((1, query_blocks, lanes), lambda h: (h, 0, 0))
    numers = [jax.ShapeDtypeStruct((qtok, width), jnp.float32)]
    if rows_each:
        numers = [jax.ShapeDtypeStruct((qtok // CORES, width), t) for t in (jnp.float32, jnp.bfloat16)]
    return pl.pallas_call(
        functools.partial(attend_kernel, rows_each),
        grid=(heads_kv,),
        out_shape=(*numers, stat, stat),
        in_specs=[
            pl.BlockSpec(memory_space=pltpu.SMEM),
            pl.BlockSpec((qtok, columns), lambda h: (0, h)),
            pl.BlockSpec((kdev, HEAD_SIZE), lambda h: (0, h)),
            pl.BlockSpec((kdev, HEAD_SIZE), lambda h: (0, h)),
        ],
        out_specs=(
            *(pl.BlockSpec((numer.shape[0], columns), lambda h: (0, h)) for numer in numers),
            stat_spec,
            stat_spec,
        ),
        scratch_shapes=[
            pltpu.SMEM((key_blocks + 2,), jnp.int32),
            pltpu.VMEM(((key_blocks + 1) // 2, 2 * kdev // key_blocks, lanes), jnp.float32),
        ],
        compiler_params=pltpu.CompilerParams(vmem_limit_bytes=60 * 2**20),
        name="attend",
    )(block_mask, whole, keys, values)


def by_token(stat, qtok):
    heads_kv, query_blocks, _ = stat.shape
    stat = stat.reshape(heads_kv, query_blocks, -1, qtok // query_blocks)
    return stat.transpose(1, 3, 0, 2).reshape(qtok, -1)


def shards_any(queries, keys, values, block_mask, out_weight):
    whole = lax.all_gather(queries, "ctx", axis=0, tiled=True)
    qtok, width = whole.shape
    numer, top, total = attend(whole, keys, values, block_mask, 0)
    rescale = by_token(jnp.exp2(top - lax.pmax(top, "ctx")), qtok)
    denom = by_token(total, qtok) * rescale
    numer = (numer.reshape(qtok, -1, HEAD_SIZE) * rescale[:, :, None]).reshape(qtok, width)
    num_rows = lax.psum_scatter(numer, "ctx", scatter_dimension=0, tiled=True)
    den_rows = lax.psum_scatter(denom, "ctx", scatter_dimension=0, tiled=True)
    own_rows = num_rows.shape[0]
    attn_rows = (num_rows.reshape(own_rows, -1, HEAD_SIZE) / den_rows[:, :, None]).reshape(
        own_rows, width
    )
    attn_cols = lax.all_to_all(
        attn_rows.astype(jnp.bfloat16), "ctx", split_axis=1, concat_axis=0, tiled=True
    )
    summed = lax.psum_scatter(
        jnp.dot(attn_cols, out_weight, preferred_element_type=jnp.float32),
        "ctx",
        scatter_dimension=0,
        tiled=True,
    )
    return summed.astype(jnp.bfloat16)


def place(n):
    me = lax.axis_index("ctx")
    core = lax.rem(me, CORES)
    x = lax.rem(me // CORES, ROW)
    plane = me // (CORES * ROW)
    return me, plane, x, core


def index_of(plane, x, core):
    return (plane * ROW + x) * CORES + core


def greet(devices):
    barrier = pltpu.get_barrier_semaphore()
    for device in devices:
        pl.semaphore_signal(barrier, inc=1, device_id={"ctx": device}, device_id_type=MESH)
    pl.semaphore_wait(barrier, len(devices))


def remote(src, dst, send, recv, device):
    return pltpu.make_async_remote_copy(
        src_ref=src,
        dst_ref=dst,
        send_sem=send,
        recv_sem=recv,
        device_id={"ctx": device},
        device_id_type=MESH,
    )


def gather_kernel(n, own_ref, whole_ref, own_sem, send_sem, recv_sem):
    me, plane, x, core = place(n)
    planes = n // (CORES * ROW)
    beside, sibling = 1 - x, 1 - core
    barrier = pltpu.get_barrier_semaphore()

    def hello(device):
        pl.semaphore_signal(barrier, inc=1, device_id={"ctx": device}, device_id_type=MESH)

    hello(index_of(plane, beside, core))
    hello(index_of(plane, x, sibling))

    @pl.when(plane > 0)
    def _():
        hello(index_of(plane - 1, x, core))

    @pl.when(plane < planes - 1)
    def _():
        hello(index_of(plane + 1, x, core))

    ends = (plane > 0).astype(jnp.int32) + (plane < planes - 1).astype(jnp.int32)
    pl.semaphore_wait(barrier, 2 + ends)
    own = pltpu.make_async_copy(own_ref, whole_ref.at[me], own_sem)
    own.start()

    def copy_to(block, way, device, mine=False):
        src = own_ref if mine else whole_ref.at[block]
        return remote(src, whole_ref.at[block], send_sem.at[way, block], recv_sem.at[block], device)

    def arrived(block):
        copy_to(block, 0, me).wait_recv()

    def pass_on(p, up, act, mine=False):
        block = index_of(p, x, core)

        @pl.when(plane + up < planes if up > 0 else plane + up >= 0)
        def _():
            act(copy_to(block, 0 if up > 0 else 1, index_of(plane + up, x, core), mine))

    start, ended = (lambda copy: copy.start()), (lambda copy: copy.wait_send())
    pass_on(plane, 1, start, True)
    pass_on(plane, -1, start, True)
    copy_to(me, 2, index_of(plane, beside, core), True).start()
    copy_to(me, 3, index_of(plane, x, sibling), True).start()
    for distance in range(1, planes):
        for up in (1, -1):
            p = plane - up * distance

            @pl.when(p >= 0 if up > 0 else p < planes)
            def _():
                block = index_of(p, x, core)
                arrived(block)
                pass_on(p, up, start)
                copy_to(block, 2, index_of(plane, beside, core)).start()
                copy_to(block, 3, index_of(plane, x, sibling)).start()

    def near_first(act):
        act(plane)
        for distance in range(1, planes):
            for up in (1, -1):
                p = plane - up * distance

                @pl.when(p >= 0 if up > 0 else p < planes)
                def _():
                    act(p)

    def from_beside(p):
        block = index_of(p, beside, core)
        arrived(block)
        copy_to(block, 3, index_of(plane, x, sibling)).start()

    def from_sibling(p):
        arrived(index_of(p, x, sibling))
        arrived(index_of(p, beside, sibling))

    near_first(from_beside)
    near_first(from_sibling)
    pass_on(plane, 1, ended, True)
    pass_on(plane, -1, ended, True)
    for distance in range(1, planes):
        for up in (1, -1):
            p = plane - up * distance

            @pl.when(p >= 0 if up > 0 else p < planes)
            def _():
                pass_on(p, up, ended)

    def sent(p):
        copy_to(index_of(p, x, core), 2, index_of(plane, beside, core)).wait_send()
        copy_to(index_of(p, x, core), 3, index_of(plane, x, sibling)).wait_send()
        copy_to(index_of(p, beside, core), 3, index_of(plane, x, sibling)).wait_send()

    near_first(sent)
    own.wait()


def gather_rows(queries, n):
    rows, width = queries.shape
    whole = pl.pallas_call(
        functools.partial(gather_kernel, n),
        out_shape=jax.ShapeDtypeStruct((n, rows, width), queries.dtype),
        in_specs=[pl.BlockSpec(memory_space=pltpu.VMEM)],
        out_specs=pl.BlockSpec(memory_space=pltpu.VMEM),
        scratch_shapes=[
            pltpu.SemaphoreType.DMA,
            pltpu.SemaphoreType.DMA((4, n)),
            pltpu.SemaphoreType.DMA((n,)),
        ],
        compiler_params=pltpu.CompilerParams(collective_id=0, has_side_effects=True),
        name="gather_rows",
    )(queries)
    return whole.reshape(n * rows, width)


def reduce_rows(place_of, parts, merge, finish):
    plane, x, core, planes = place_of
    beside, sibling = 1 - x, 1 - core
    others = [lax.rem(plane + step, planes) for step in range(1, planes)]

    def turn(step):
        return lax.rem(plane + 1 + step, planes)

    def core_copy(part, p):
        sem = part[9]
        return remote(
            part[0](p), part[2].at[p], sem.at[0, p], sem.at[1, p], index_of(plane, x, sibling)
        )

    def beside_copy(part, p):
        sem = part[9]
        return remote(
            part[3].at[p], part[5].at[p], sem.at[2, p], sem.at[3, p], index_of(plane, beside, core)
        )

    def plane_copy(part, p, slot):
        sem = part[9]
        return remote(
            part[6].at[p], part[8].at[slot], sem.at[4, p], sem.at[5, slot], index_of(p, x, core)
        )

    for p in others + [plane]:
        for part in parts:
            core_copy(part, p).start()

    def from_core(step, _):
        p = turn(step)
        for part in parts:
            core_copy(part, p).wait_recv()
        for side, out in ((beside, 3), (x, 4)):
            merge(
                [part[1](p, side) for part in parts],
                [part[2].at[p, side] for part in parts],
                [part[out].at[p] for part in parts],
            )
            if out == 3:
                for part in parts:
                    beside_copy(part, p).start()
        return 0

    lax.fori_loop(0, planes, from_core, 0)

    def from_beside(p, outs):
        for part in parts:
            beside_copy(part, p).wait_recv()
        merge([part[4].at[p] for part in parts], [part[5].at[p] for part in parts], outs)

    def to_plane(step, _):
        p = turn(step)
        from_beside(p, [part[6].at[p] for part in parts])
        for part in parts:
            plane_copy(part, p, plane).start()
        return 0

    lax.fori_loop(0, planes - 1, to_plane, 0)
    from_beside(plane, [part[7] for part in parts])
    for p in others:
        for part in parts:
            plane_copy(part, p, p).wait_recv()
    finish([[part[7] for part in parts]] + [[part[8].at[p] for part in parts] for p in others])
    for p in others + [plane]:
        for part in parts:
            core_copy(part, p).wait_send()
            beside_copy(part, p).wait_send()
    for p in others:
        for part in parts:
            plane_copy(part, p, plane).wait_send()


def reduce_scratch(planes, rows, width, dtype):
    return [
        pltpu.VMEM((planes, ROW, rows, width), dtype),
        pltpu.VMEM((planes, rows, width), dtype),
        pltpu.VMEM((planes, rows, width), jnp.float32),
        pltpu.VMEM((planes, rows, width), dtype),
        pltpu.VMEM((planes, rows, width), dtype),
        pltpu.VMEM((rows, width), jnp.float32),
        pltpu.VMEM((planes, rows, width), dtype),
        pltpu.SemaphoreType.DMA((6, planes)),
    ]


STATS = 128


def weigh(stats):
    half = STATS // 2
    tops = [stat[:, :half] for stat in stats]
    top = functools.reduce(jnp.maximum, tops)
    factors = [jnp.exp2(one - top) for one in tops]
    total = sum(stat[:, half:] * factor for stat, factor in zip(stats, factors))
    return top, factors, total


def combine_kernel(n, kept_ref, sent_ref, stat_ref, cols_ref, *scratch):
    numer_scratch, stat_scratch = scratch[:8], scratch[8:16]
    piece_ref, swap_send, swap_recv, own_sem = scratch[16:]
    me, plane, x, core = place(n)
    planes = n // (CORES * ROW)
    width = kept_ref.shape[-1]
    heads = width // HEAD_SIZE
    others = [lax.rem(me + step, n) for step in range(1, n)]
    greet(others)

    def merge(one, two, out):
        top, factors, total = weigh([one[1][...], two[1][...]])
        out[1][...] = jnp.concatenate([top, total], axis=1)
        for head in range(heads):
            at = slice(head * HEAD_SIZE, (head + 1) * HEAD_SIZE)
            out[0][:, at] = (
                one[0][:, at].astype(jnp.float32) * factors[0][:, head : head + 1]
                + two[0][:, at].astype(jnp.float32) * factors[1][:, head : head + 1]
            ).astype(out[0].dtype)

    def finish(sources):
        _, factors, total = weigh([source[1][...] for source in sources])
        out = []
        for head in range(heads):
            at = slice(head * HEAD_SIZE, (head + 1) * HEAD_SIZE)
            numer = sum(
                source[0][:, at].astype(jnp.float32) * factor[:, head : head + 1]
                for source, factor in zip(sources, factors)
            )
            out.append((numer / total[:, head : head + 1]).astype(jnp.bfloat16))
        attn = jnp.concatenate(out, axis=1)
        share = width // n
        for device in range(n):
            piece_ref[device] = attn[:, device * share : (device + 1) * share]

    reduce_rows(
        (plane, x, core, planes),
        [
            (lambda p: sent_ref.at[p], lambda p, side: kept_ref.at[p, side], *numer_scratch),
            (
                lambda p: stat_ref.at[p, :, 1 - core],
                lambda p, side: stat_ref.at[p, side, core],
                *stat_scratch,
            ),
        ],
        merge,
        finish,
    )

    def swap(device, slot):
        return remote(
            piece_ref.at[device], cols_ref.at[slot], swap_send.at[device], swap_recv.at[slot], device
        )

    own = pltpu.make_async_copy(piece_ref.at[me], cols_ref.at[me], own_sem)
    own.start()
    for device in others:
        swap(device, me).start()
    own.wait()
    for device in others:
        swap(device, device).wait_recv()
    for device in others:
        swap(device, me).wait_send()


def combine(kept, sent, stats, n):
    qtok, width = stats.shape[0], kept.shape[1]
    planes, rows = n // (CORES * ROW), qtok // n
    cols = pl.pallas_call(
        functools.partial(combine_kernel, n),
        out_shape=jax.ShapeDtypeStruct((n, rows, width // n), jnp.bfloat16),
        in_specs=[pl.BlockSpec(memory_space=pltpu.VMEM)] * 3,
        out_specs=pl.BlockSpec(memory_space=pltpu.VMEM),
        scratch_shapes=reduce_scratch(planes, rows, width, jnp.bfloat16)
        + reduce_scratch(planes, rows, STATS, jnp.float32)
        + [
            pltpu.VMEM((n, rows, width // n), jnp.bfloat16),
            pltpu.SemaphoreType.DMA((n,)),
            pltpu.SemaphoreType.DMA((n,)),
            pltpu.SemaphoreType.DMA,
        ],
        compiler_params=pltpu.CompilerParams(
            collective_id=1, has_side_effects=True, vmem_limit_bytes=40 * 2**20
        ),
        name="combine",
    )(
        kept.reshape(planes, ROW, rows, width),
        sent.reshape(planes, ROW, rows, width),
        stats.reshape(planes, ROW, CORES, rows, STATS),
    )
    return cols.reshape(qtok, width // n)


TILE = 512


def project_kernel(n, cols_ref, weight_ref, out_ref, kept_ref, sent_ref, *scratch):
    _, plane, x, core = place(n)
    planes = n // (CORES * ROW)
    rows, width = out_ref.shape
    greet(
        [index_of(lax.rem(plane + step, planes), x, core) for step in range(1, planes)]
        + [index_of(plane, 1 - x, core), index_of(plane, x, 1 - core)]
    )

    def tile_step(tile, _):
        at = pl.ds(pl.multiple_of(tile * TILE, TILE), TILE)
        product = jnp.dot(cols_ref[...], weight_ref[:, at], preferred_element_type=jnp.float32)
        product = product.reshape(planes, ROW, CORES, rows, TILE)
        kept_ref[:, :, :, at] = jnp.where(core == 0, product[:, :, 0], product[:, :, 1])
        sent = jnp.where(core == 0, product[:, :, 1], product[:, :, 0])
        sent_ref[:, :, :, at] = sent.astype(sent_ref.dtype)
        return 0

    lax.fori_loop(0, width // TILE, tile_step, 0)

    def merge(one, two, out):
        out[0][...] = (one[0][...].astype(jnp.float32) + two[0][...].astype(jnp.float32)).astype(
            out[0].dtype
        )

    def finish(sources):
        out_ref[...] = sum(source[0][...].astype(jnp.float32) for source in sources).astype(
            out_ref.dtype
        )

    reduce_rows((plane, x, core, planes), [(lambda p: sent_ref.at[p], lambda p, side: kept_ref.at[p, side], *scratch)], merge, finish)


def project(cols, weight, n):
    qtok = cols.shape[0]
    width = weight.shape[1]
    planes, rows = n // (CORES * ROW), qtok // n
    return pl.pallas_call(
        functools.partial(project_kernel, n),
        out_shape=jax.ShapeDtypeStruct((rows, width), jnp.bfloat16),
        in_specs=[pl.BlockSpec(memory_space=pltpu.VMEM)] * 2,
        out_specs=pl.BlockSpec(memory_space=pltpu.VMEM),
        scratch_shapes=[pltpu.VMEM((planes, ROW, rows, width), t) for t in (jnp.float32, jnp.bfloat16)]
        + reduce_scratch(planes, rows, width, jnp.bfloat16),
        compiler_params=pltpu.CompilerParams(
            collective_id=2, has_side_effects=True, vmem_limit_bytes=40 * 2**20
        ),
        name="project",
    )(cols, weight)


def shards_near(n, queries, keys, values, block_mask, out_weight):
    whole = gather_rows(queries, n)
    qtok = whole.shape[0]
    kept, sent, top, total = attend(whole, keys, values, block_mask, queries.shape[0])
    top, total = by_token(top, qtok), by_token(total, qtok)
    room = ((0, 0), (0, STATS // 2 - top.shape[1]))
    stats = jnp.concatenate([jnp.pad(top, room), jnp.pad(total, room)], axis=1)
    cols = combine(kept, sent, stats, n)
    return project(cols, out_weight, n)


def solution(mesh):
    n = mesh.shape["ctx"]

    def shards(queries, *rest):
        fits = n % (CORES * ROW) == 0 and queries.shape[0] == 16
        if fits and queries.shape[1] // HEAD_SIZE <= STATS // 2:
            return shards_near(n, queries, *rest)
        return shards_any(queries, *rest)

    return jax.shard_map(
        shards,
        mesh=mesh,
        in_specs=(
            P(("groups", "ctx"), None),
            P(("groups", "ctx"), None),
            P(("groups", "ctx"), None),
            P("groups", None, "ctx"),
            P("ctx", None),
        ),
        out_specs=P(("groups", "ctx"), None),
        check_vma=False,
    )
```

```python
import functools
import math

import jax
import jax.numpy as jnp
from jax import lax
from jax.experimental import pallas as pl
from jax.experimental.pallas import tpu as pltpu
from jax.sharding import PartitionSpec as P

HEAD_SIZE = 128
NEG = -1e30
ONES = 16
LOG2E = math.log2(math.e)
MESH = pl.DeviceIdType.MESH
CORES, ROW = 2, 2


def attend_kernel(rows_each, mask_ref, q_ref, k_ref, v_ref, *refs):
    *numer_refs, top_ref, total_ref, live_ref, score_ref, query_ref, value_ref, sum_ref = refs
    head = pl.program_id(0)
    query_blocks, key_blocks = mask_ref.shape[1:]
    key_block = k_ref.shape[0] // key_blocks
    query_block = q_ref.shape[0] // query_blocks
    group = q_ref.shape[1] // HEAD_SIZE
    factor = LOG2E / math.sqrt(HEAD_SIZE)
    value_ref[:HEAD_SIZE] = v_ref[...].T
    value_ref[HEAD_SIZE:] = jnp.ones((ONES, v_ref.shape[0]), jnp.bfloat16)
    for at in range(query_blocks):
        rows = pl.ds(at * query_block, query_block)
        count = jnp.int32(0)
        for block in range(key_blocks):
            live_ref[count] = block
            count = count + (mask_ref[head, at, block] > 0).astype(jnp.int32)
        live_ref[count] = 0
        for g in range(group):
            tokens = q_ref[rows, g * HEAD_SIZE : (g + 1) * HEAD_SIZE]
            query_ref[:, g * query_block : (g + 1) * query_block] = tokens.T
        lanes = query_ref.shape[1]
        pairs = (count + 1) // 2

        def start_of(which):
            return pl.multiple_of(live_ref[which] * key_block, key_block)

        def score_step(pair, top):
            tops = [top]
            for half in range(2):
                block = k_ref[pl.ds(start_of(2 * pair + half), key_block), :]
                scores = jnp.dot(block, query_ref[...], preferred_element_type=jnp.float32)
                score_ref[pair, half * key_block : (half + 1) * key_block] = scores
                tops.append(jnp.max(scores.reshape(key_block // 8, 8, lanes), axis=0))
            tops[2] = jnp.where(2 * pair + 1 < count, tops[2], NEG)
            return jnp.maximum(tops[0], jnp.maximum(tops[1], tops[2]))

        top = lax.fori_loop(0, pairs, score_step, jnp.full((8, lanes), NEG, jnp.float32))
        top = jnp.max(top, axis=0, keepdims=True) * factor
        sum_ref[...] = jnp.zeros_like(sum_ref)

        def sum_step(pair, _):
            shifts = [top, jnp.where(2 * pair + 1 < count, top, -NEG)]
            probs = [
                jnp.exp2(score_ref[pair, half * key_block : (half + 1) * key_block] * factor - shift)
                for half, shift in enumerate(shifts)
            ]
            probs = jnp.concatenate([one.astype(jnp.bfloat16) for one in probs], axis=0)
            both = [value_ref[:, pl.ds(start_of(2 * pair + half), key_block)] for half in range(2)]
            sum_ref[...] += jnp.dot(
                jnp.concatenate(both, axis=1), probs, preferred_element_type=jnp.float32
            )
            return 0

        lax.fori_loop(0, pairs, sum_step, 0)
        numer = sum_ref[:HEAD_SIZE]
        top_ref[0, at : at + 1, :] = top
        total_ref[0, at : at + 1, :] = sum_ref[HEAD_SIZE : HEAD_SIZE + 1]
        for g in range(group):
            columns = slice(g * query_block, (g + 1) * query_block)
            out_columns = slice(g * HEAD_SIZE, (g + 1) * HEAD_SIZE)
            tokens = numer[:, columns].T
            if not rows_each:
                numer_refs[0][rows, out_columns] = tokens
                continue
            tokens = tokens.reshape(-1, CORES, rows_each, HEAD_SIZE)
            first = lax.rem(lax.axis_index("ctx"), CORES) == 0
            half = pl.ds(at * query_block // CORES, query_block // CORES)
            kept = jnp.where(first, tokens[:, 0], tokens[:, 1]).reshape(-1, HEAD_SIZE)
            sent = jnp.where(first, tokens[:, 1], tokens[:, 0]).reshape(-1, HEAD_SIZE)
            numer_refs[0][half, out_columns] = kept
            numer_refs[1][half, out_columns] = sent.astype(jnp.bfloat16)


def attend(whole, keys, values, block_mask, rows_each):
    qtok, width = whole.shape
    kdev = keys.shape[0]
    heads_kv, query_blocks, key_blocks = block_mask.shape
    columns = width // heads_kv
    lanes = columns // HEAD_SIZE * (qtok // query_blocks)
    stat = jax.ShapeDtypeStruct((heads_kv, query_blocks, lanes), jnp.float32)
    stat_spec = pl.BlockSpec((1, query_blocks, lanes), lambda h: (h, 0, 0))
    numers = [jax.ShapeDtypeStruct((qtok, width), jnp.float32)]
    if rows_each:
        numers = [jax.ShapeDtypeStruct((qtok // CORES, width), t) for t in (jnp.float32, jnp.bfloat16)]
    return pl.pallas_call(
        functools.partial(attend_kernel, rows_each),
        grid=(heads_kv,),
        out_shape=(*numers, stat, stat),
        in_specs=[
            pl.BlockSpec(memory_space=pltpu.SMEM),
            pl.BlockSpec((qtok, columns), lambda h: (0, h)),
            pl.BlockSpec((kdev, HEAD_SIZE), lambda h: (0, h)),
            pl.BlockSpec((kdev, HEAD_SIZE), lambda h: (0, h)),
        ],
        out_specs=(
            *(pl.BlockSpec((numer.shape[0], columns), lambda h: (0, h)) for numer in numers),
            stat_spec,
            stat_spec,
        ),
        scratch_shapes=[
            pltpu.SMEM((key_blocks + 2,), jnp.int32),
            pltpu.VMEM(((key_blocks + 1) // 2, 2 * kdev // key_blocks, lanes), jnp.float32),
            pltpu.VMEM((HEAD_SIZE, lanes), jnp.bfloat16),
            pltpu.VMEM((HEAD_SIZE + ONES, kdev), jnp.bfloat16),
            pltpu.VMEM((HEAD_SIZE + ONES, lanes), jnp.float32),
        ],
        compiler_params=pltpu.CompilerParams(vmem_limit_bytes=60 * 2**20),
        name="attend",
    )(block_mask, whole, keys, values)


def by_token(stat, qtok):
    heads_kv, query_blocks, _ = stat.shape
    stat = stat.reshape(heads_kv, query_blocks, -1, qtok // query_blocks)
    return stat.transpose(1, 3, 0, 2).reshape(qtok, -1)


def shards_any(queries, keys, values, block_mask, out_weight):
    whole = lax.all_gather(queries, "ctx", axis=0, tiled=True)
    qtok, width = whole.shape
    numer, top, total = attend(whole, keys, values, block_mask, 0)
    rescale = by_token(jnp.exp2(top - lax.pmax(top, "ctx")), qtok)
    denom = by_token(total, qtok) * rescale
    numer = (numer.reshape(qtok, -1, HEAD_SIZE) * rescale[:, :, None]).reshape(qtok, width)
    num_rows = lax.psum_scatter(numer, "ctx", scatter_dimension=0, tiled=True)
    den_rows = lax.psum_scatter(denom, "ctx", scatter_dimension=0, tiled=True)
    own_rows = num_rows.shape[0]
    attn_rows = (num_rows.reshape(own_rows, -1, HEAD_SIZE) / den_rows[:, :, None]).reshape(
        own_rows, width
    )
    attn_cols = lax.all_to_all(
        attn_rows.astype(jnp.bfloat16), "ctx", split_axis=1, concat_axis=0, tiled=True
    )
    summed = lax.psum_scatter(
        jnp.dot(attn_cols, out_weight, preferred_element_type=jnp.float32),
        "ctx",
        scatter_dimension=0,
        tiled=True,
    )
    return summed.astype(jnp.bfloat16)


def place(n):
    me = lax.axis_index("ctx")
    core = lax.rem(me, CORES)
    x = lax.rem(me // CORES, ROW)
    plane = me // (CORES * ROW)
    return me, plane, x, core


def index_of(plane, x, core):
    return (plane * ROW + x) * CORES + core


def greet(devices):
    barrier = pltpu.get_barrier_semaphore()
    for device in devices:
        pl.semaphore_signal(barrier, inc=1, device_id={"ctx": device}, device_id_type=MESH)
    pl.semaphore_wait(barrier, len(devices))


def remote(src, dst, send, recv, device):
    return pltpu.make_async_remote_copy(
        src_ref=src,
        dst_ref=dst,
        send_sem=send,
        recv_sem=recv,
        device_id={"ctx": device},
        device_id_type=MESH,
    )


def gather_kernel(n, own_ref, whole_ref, own_sem, send_sem, recv_sem):
    me, plane, x, core = place(n)
    planes = n // (CORES * ROW)
    beside, sibling = 1 - x, 1 - core
    barrier = pltpu.get_barrier_semaphore()

    def hello(device):
        pl.semaphore_signal(barrier, inc=1, device_id={"ctx": device}, device_id_type=MESH)

    hello(index_of(plane, beside, core))
    hello(index_of(plane, x, sibling))

    @pl.when(plane > 0)
    def _():
        hello(index_of(plane - 1, x, core))

    @pl.when(plane < planes - 1)
    def _():
        hello(index_of(plane + 1, x, core))

    ends = (plane > 0).astype(jnp.int32) + (plane < planes - 1).astype(jnp.int32)
    pl.semaphore_wait(barrier, 2 + ends)
    own = pltpu.make_async_copy(own_ref, whole_ref.at[me], own_sem)
    own.start()

    def copy_to(block, way, device, mine=False):
        src = own_ref if mine else whole_ref.at[block]
        return remote(src, whole_ref.at[block], send_sem.at[way, block], recv_sem.at[block], device)

    def arrived(block):
        copy_to(block, 0, me).wait_recv()

    def pass_on(p, up, act, mine=False):
        block = index_of(p, x, core)

        @pl.when(plane + up < planes if up > 0 else plane + up >= 0)
        def _():
            act(copy_to(block, 0 if up > 0 else 1, index_of(plane + up, x, core), mine))

    start, ended = (lambda copy: copy.start()), (lambda copy: copy.wait_send())
    pass_on(plane, 1, start, True)
    pass_on(plane, -1, start, True)
    copy_to(me, 2, index_of(plane, beside, core), True).start()
    copy_to(me, 3, index_of(plane, x, sibling), True).start()
    for distance in range(1, planes):
        for up in (1, -1):
            p = plane - up * distance

            @pl.when(p >= 0 if up > 0 else p < planes)
            def _():
                block = index_of(p, x, core)
                arrived(block)
                pass_on(p, up, start)
                copy_to(block, 2, index_of(plane, beside, core)).start()
                copy_to(block, 3, index_of(plane, x, sibling)).start()

    def near_first(act):
        act(plane)
        for distance in range(1, planes):
            for up in (1, -1):
                p = plane - up * distance

                @pl.when(p >= 0 if up > 0 else p < planes)
                def _():
                    act(p)

    def from_beside(p):
        block = index_of(p, beside, core)
        arrived(block)
        copy_to(block, 3, index_of(plane, x, sibling)).start()

    def from_sibling(p):
        arrived(index_of(p, x, sibling))
        arrived(index_of(p, beside, sibling))

    near_first(from_beside)
    near_first(from_sibling)
    pass_on(plane, 1, ended, True)
    pass_on(plane, -1, ended, True)
    for distance in range(1, planes):
        for up in (1, -1):
            p = plane - up * distance

            @pl.when(p >= 0 if up > 0 else p < planes)
            def _():
                pass_on(p, up, ended)

    def sent(p):
        copy_to(index_of(p, x, core), 2, index_of(plane, beside, core)).wait_send()
        copy_to(index_of(p, x, core), 3, index_of(plane, x, sibling)).wait_send()
        copy_to(index_of(p, beside, core), 3, index_of(plane, x, sibling)).wait_send()

    near_first(sent)
    own.wait()


def gather_rows(queries, n):
    rows, width = queries.shape
    whole = pl.pallas_call(
        functools.partial(gather_kernel, n),
        out_shape=jax.ShapeDtypeStruct((n, rows, width), queries.dtype),
        in_specs=[pl.BlockSpec(memory_space=pltpu.VMEM)],
        out_specs=pl.BlockSpec(memory_space=pltpu.VMEM),
        scratch_shapes=[
            pltpu.SemaphoreType.DMA,
            pltpu.SemaphoreType.DMA((4, n)),
            pltpu.SemaphoreType.DMA((n,)),
        ],
        compiler_params=pltpu.CompilerParams(collective_id=0, has_side_effects=True),
        name="gather_rows",
    )(queries)
    return whole.reshape(n * rows, width)


def reduce_rows(place_of, parts, merge, finish):
    plane, x, core, planes = place_of
    beside, sibling = 1 - x, 1 - core
    others = [lax.rem(plane + step, planes) for step in range(1, planes)]

    def turn(step):
        return lax.rem(plane + 1 + step, planes)

    def core_copy(part, p):
        sem = part[9]
        return remote(
            part[0](p), part[2].at[p], sem.at[0, p], sem.at[1, p], index_of(plane, x, sibling)
        )

    def beside_copy(part, p):
        sem = part[9]
        return remote(
            part[3].at[p], part[5].at[p], sem.at[2, p], sem.at[3, p], index_of(plane, beside, core)
        )

    def plane_copy(part, p, slot):
        sem = part[9]
        return remote(
            part[6].at[p], part[8].at[slot], sem.at[4, p], sem.at[5, slot], index_of(p, x, core)
        )

    for p in others + [plane]:
        for part in parts:
            core_copy(part, p).start()

    def from_core(step, _):
        p = turn(step)
        for part in parts:
            core_copy(part, p).wait_recv()
        for side, out in ((beside, 3), (x, 4)):
            merge(
                [part[1](p, side) for part in parts],
                [part[2].at[p, side] for part in parts],
                [part[out].at[p] for part in parts],
            )
            if out == 3:
                for part in parts:
                    beside_copy(part, p).start()
        return 0

    lax.fori_loop(0, planes, from_core, 0)

    def from_beside(p, outs):
        for part in parts:
            beside_copy(part, p).wait_recv()
        merge([part[4].at[p] for part in parts], [part[5].at[p] for part in parts], outs)

    def to_plane(step, _):
        p = turn(step)
        from_beside(p, [part[6].at[p] for part in parts])
        for part in parts:
            plane_copy(part, p, plane).start()
        return 0

    lax.fori_loop(0, planes - 1, to_plane, 0)
    from_beside(plane, [part[7] for part in parts])
    for p in others:
        for part in parts:
            plane_copy(part, p, p).wait_recv()
    finish([[part[7] for part in parts]] + [[part[8].at[p] for part in parts] for p in others])
    for p in others + [plane]:
        for part in parts:
            core_copy(part, p).wait_send()
            beside_copy(part, p).wait_send()
    for p in others:
        for part in parts:
            plane_copy(part, p, plane).wait_send()


def reduce_scratch(planes, rows, width, dtype):
    return [
        pltpu.VMEM((planes, ROW, rows, width), dtype),
        pltpu.VMEM((planes, rows, width), dtype),
        pltpu.VMEM((planes, rows, width), jnp.float32),
        pltpu.VMEM((planes, rows, width), dtype),
        pltpu.VMEM((planes, rows, width), dtype),
        pltpu.VMEM((rows, width), jnp.float32),
        pltpu.VMEM((planes, rows, width), dtype),
        pltpu.SemaphoreType.DMA((6, planes)),
    ]


STATS = 128


def weigh(stats):
    half = STATS // 2
    tops = [stat[:, :half] for stat in stats]
    top = functools.reduce(jnp.maximum, tops)
    factors = [jnp.exp2(one - top) for one in tops]
    total = sum(stat[:, half:] * factor for stat, factor in zip(stats, factors))
    return top, factors, total


def combine_kernel(n, kept_hbm, sent_ref, stat_ref, cols_ref, *scratch):
    numer_scratch, stat_scratch = scratch[:8], scratch[8:16]
    piece_ref, swap_send, swap_recv, own_sem, kept_ref, kept_sem = scratch[16:]
    keep = pltpu.make_async_copy(kept_hbm, kept_ref, kept_sem)
    keep.start()
    me, plane, x, core = place(n)
    planes = n // (CORES * ROW)
    width = kept_ref.shape[-1]
    heads = width // HEAD_SIZE
    others = [lax.rem(me + step, n) for step in range(1, n)]
    greet(others)
    keep.wait()

    def merge(one, two, out):
        top, factors, total = weigh([one[1][...], two[1][...]])
        out[1][...] = jnp.concatenate([top, total], axis=1)
        for head in range(heads):
            at = slice(head * HEAD_SIZE, (head + 1) * HEAD_SIZE)
            out[0][:, at] = (
                one[0][:, at].astype(jnp.float32) * factors[0][:, head : head + 1]
                + two[0][:, at].astype(jnp.float32) * factors[1][:, head : head + 1]
            ).astype(out[0].dtype)

    def finish(sources):
        _, factors, total = weigh([source[1][...] for source in sources])
        out = []
        for head in range(heads):
            at = slice(head * HEAD_SIZE, (head + 1) * HEAD_SIZE)
            numer = sum(
                source[0][:, at].astype(jnp.float32) * factor[:, head : head + 1]
                for source, factor in zip(sources, factors)
            )
            out.append((numer / total[:, head : head + 1]).astype(jnp.bfloat16))
        attn = jnp.concatenate(out, axis=1)
        share = width // n
        for device in range(n):
            piece_ref[device] = attn[:, device * share : (device + 1) * share]

    reduce_rows(
        (plane, x, core, planes),
        [
            (lambda p: sent_ref.at[p], lambda p, side: kept_ref.at[p, side], *numer_scratch),
            (
                lambda p: stat_ref.at[p, :, 1 - core],
                lambda p, side: stat_ref.at[p, side, core],
                *stat_scratch,
            ),
        ],
        merge,
        finish,
    )

    def swap(device, slot):
        return remote(
            piece_ref.at[device], cols_ref.at[slot], swap_send.at[device], swap_recv.at[slot], device
        )

    own = pltpu.make_async_copy(piece_ref.at[me], cols_ref.at[me], own_sem)
    own.start()
    for device in others:
        swap(device, me).start()
    own.wait()
    for device in others:
        swap(device, device).wait_recv()
    for device in others:
        swap(device, me).wait_send()


def combine(kept, sent, stats, n):
    qtok, width = stats.shape[0], kept.shape[1]
    planes, rows = n // (CORES * ROW), qtok // n
    cols = pl.pallas_call(
        functools.partial(combine_kernel, n),
        out_shape=jax.ShapeDtypeStruct((n, rows, width // n), jnp.bfloat16),
        in_specs=[pl.BlockSpec(memory_space=pl.ANY)] * 2
        + [pl.BlockSpec(memory_space=pltpu.VMEM)],
        out_specs=pl.BlockSpec(memory_space=pltpu.VMEM),
        scratch_shapes=reduce_scratch(planes, rows, width, jnp.bfloat16)
        + reduce_scratch(planes, rows, STATS, jnp.float32)
        + [
            pltpu.VMEM((n, rows, width // n), jnp.bfloat16),
            pltpu.SemaphoreType.DMA((n,)),
            pltpu.SemaphoreType.DMA((n,)),
            pltpu.SemaphoreType.DMA,
            pltpu.VMEM((planes, ROW, rows, width), jnp.float32),
            pltpu.SemaphoreType.DMA,
        ],
        compiler_params=pltpu.CompilerParams(
            collective_id=1, has_side_effects=True, vmem_limit_bytes=60 * 2**20
        ),
        name="combine",
    )(
        kept.reshape(planes, ROW, rows, width),
        sent.reshape(planes, ROW, rows, width),
        stats.reshape(planes, ROW, CORES, rows, STATS),
    )
    return cols.reshape(qtok, width // n)


TILE = 512


def project_kernel(n, cols_ref, weight_hbm, out_ref, weight_ref, weight_sem, kept_ref, sent_ref, *scratch):
    _, plane, x, core = place(n)
    planes = n // (CORES * ROW)
    rows, width = out_ref.shape

    def fetch(tile):
        at = pl.ds(pl.multiple_of(tile * TILE, TILE), TILE)
        return pltpu.make_async_copy(weight_hbm.at[:, at], weight_ref.at[:, at], weight_sem.at[tile])

    for tile in range(width // TILE):
        fetch(tile).start()
    greet(
        [index_of(lax.rem(plane + step, planes), x, core) for step in range(1, planes)]
        + [index_of(plane, 1 - x, core), index_of(plane, x, 1 - core)]
    )

    def tile_step(tile, _):
        at = pl.ds(pl.multiple_of(tile * TILE, TILE), TILE)
        fetch(tile).wait()
        product = jnp.dot(cols_ref[...], weight_ref[:, at], preferred_element_type=jnp.float32)
        product = product.reshape(planes, ROW, CORES, rows, TILE)
        kept_ref[:, :, :, at] = jnp.where(core == 0, product[:, :, 0], product[:, :, 1])
        sent = jnp.where(core == 0, product[:, :, 1], product[:, :, 0])
        sent_ref[:, :, :, at] = sent.astype(sent_ref.dtype)
        return 0

    lax.fori_loop(0, width // TILE, tile_step, 0)

    def merge(one, two, out):
        out[0][...] = (one[0][...].astype(jnp.float32) + two[0][...].astype(jnp.float32)).astype(
            out[0].dtype
        )

    def finish(sources):
        out_ref[...] = sum(source[0][...].astype(jnp.float32) for source in sources).astype(
            out_ref.dtype
        )

    reduce_rows((plane, x, core, planes), [(lambda p: sent_ref.at[p], lambda p, side: kept_ref.at[p, side], *scratch)], merge, finish)


def project(cols, weight, n):
    qtok = cols.shape[0]
    width = weight.shape[1]
    planes, rows = n // (CORES * ROW), qtok // n
    return pl.pallas_call(
        functools.partial(project_kernel, n),
        out_shape=jax.ShapeDtypeStruct((rows, width), jnp.bfloat16),
        in_specs=[pl.BlockSpec(memory_space=pltpu.VMEM), pl.BlockSpec(memory_space=pl.ANY)],
        out_specs=pl.BlockSpec(memory_space=pltpu.VMEM),
        scratch_shapes=[
            pltpu.VMEM(weight.shape, weight.dtype),
            pltpu.SemaphoreType.DMA((width // TILE,)),
        ]
        + [pltpu.VMEM((planes, ROW, rows, width), t) for t in (jnp.float32, jnp.bfloat16)]
        + reduce_scratch(planes, rows, width, jnp.bfloat16),
        compiler_params=pltpu.CompilerParams(
            collective_id=2, has_side_effects=True, vmem_limit_bytes=60 * 2**20
        ),
        name="project",
    )(cols, weight)


def shards_near(n, queries, keys, values, block_mask, out_weight):
    whole = gather_rows(queries, n)
    qtok = whole.shape[0]
    kept, sent, top, total = attend(whole, keys, values, block_mask, queries.shape[0])
    top, total = by_token(top, qtok), by_token(total, qtok)
    room = ((0, 0), (0, STATS // 2 - top.shape[1]))
    stats = jnp.concatenate([jnp.pad(top, room), jnp.pad(total, room)], axis=1)
    cols = combine(kept, sent, stats, n)
    return project(cols, out_weight, n)


def solution(mesh):
    n = mesh.shape["ctx"]

    def shards(queries, *rest):
        fits = n % (CORES * ROW) == 0 and queries.shape[0] == 16
        if fits and queries.shape[1] // HEAD_SIZE <= STATS // 2:
            return shards_near(n, queries, *rest)
        return shards_any(queries, *rest)

    return jax.shard_map(
        shards,
        mesh=mesh,
        in_specs=(
            P(("groups", "ctx"), None),
            P(("groups", "ctx"), None),
            P(("groups", "ctx"), None),
            P("groups", None, "ctx"),
            P("ctx", None),
        ),
        out_specs=P(("groups", "ctx"), None),
        check_vma=False,
    )
```

```python
import functools
import math

import jax
import jax.numpy as jnp
from jax import lax
from jax.experimental import pallas as pl
from jax.experimental.pallas import tpu as pltpu
from jax.sharding import PartitionSpec as P

HEAD_SIZE = 128
NEG = -1e30
ONES = 16
LOG2E = math.log2(math.e)
MESH = pl.DeviceIdType.MESH
CORES, ROW = 2, 2


def attend_kernel(rows_each, mask_ref, q_ref, k_ref, v_ref, *refs):
    *numer_refs, top_ref, total_ref, live_ref, score_ref, query_ref, value_ref, sum_ref = refs
    head = pl.program_id(0)
    query_blocks, key_blocks = mask_ref.shape[1:]
    key_block = k_ref.shape[0] // key_blocks
    query_block = q_ref.shape[0] // query_blocks
    group = q_ref.shape[1] // HEAD_SIZE
    factor = LOG2E / math.sqrt(HEAD_SIZE)
    value_ref[:HEAD_SIZE] = v_ref[...].T
    value_ref[HEAD_SIZE:] = jnp.ones((ONES, v_ref.shape[0]), jnp.bfloat16)
    for at in range(query_blocks):
        rows = pl.ds(at * query_block, query_block)
        count = jnp.int32(0)
        for block in range(key_blocks):
            live_ref[count] = block
            count = count + (mask_ref[head, at, block] > 0).astype(jnp.int32)
        live_ref[count] = 0
        for g in range(group):
            tokens = q_ref[rows, g * HEAD_SIZE : (g + 1) * HEAD_SIZE]
            query_ref[:, g * query_block : (g + 1) * query_block] = tokens.T
        lanes = query_ref.shape[1]
        pairs = (count + 1) // 2

        def start_of(which):
            return pl.multiple_of(live_ref[which] * key_block, key_block)

        quads = count // 4

        def taken(ref_slice, first, blocks, axis):
            return jnp.concatenate([ref_slice(start_of(first + b)) for b in range(blocks)], axis=axis)

        def score_step(blocks, step, top):
            pair = step * (blocks // 2)
            keys = taken(lambda at: k_ref[pl.ds(at, key_block), :], 2 * pair, blocks, 0)
            scores = jnp.dot(keys, query_ref[...], preferred_element_type=jnp.float32)
            score_ref[pl.ds(pair, blocks // 2)] = scores.reshape(blocks // 2, 2 * key_block, lanes)
            tops = jnp.max(scores.reshape(blocks, key_block // 8, 8, lanes), axis=1)
            for b in range(blocks):
                one = tops[b]
                if b == blocks - 1:
                    one = jnp.where(2 * pair + b < count, one, NEG)
                top = jnp.maximum(top, one)
            return top

        top = jnp.full((8, lanes), NEG, jnp.float32)
        top = lax.fori_loop(0, quads, functools.partial(score_step, 4), top)
        top = lax.fori_loop(2 * quads, pairs, functools.partial(score_step, 2), top)
        top = jnp.max(top, axis=0, keepdims=True) * factor
        sum_ref[...] = jnp.zeros_like(sum_ref)

        def sum_step(blocks, step, _):
            pair = step * (blocks // 2)
            probs = []
            for b in range(blocks):
                shift = top
                if b == blocks - 1:
                    shift = jnp.where(2 * pair + b < count, top, -NEG)
                half = slice(b % 2 * key_block, (b % 2 + 1) * key_block)
                scores = score_ref[pair + b // 2, half]
                probs.append(jnp.exp2(scores * factor - shift).astype(jnp.bfloat16))
            values = taken(lambda at: value_ref[:, pl.ds(at, key_block)], 2 * pair, blocks, 1)
            sum_ref[...] += jnp.dot(
                values, jnp.concatenate(probs, axis=0), preferred_element_type=jnp.float32
            )
            return 0

        lax.fori_loop(0, quads, functools.partial(sum_step, 4), 0)
        lax.fori_loop(2 * quads, pairs, functools.partial(sum_step, 2), 0)
        numer = sum_ref[:HEAD_SIZE]
        top_ref[0, at : at + 1, :] = top
        total_ref[0, at : at + 1, :] = sum_ref[HEAD_SIZE : HEAD_SIZE + 1]
        for g in range(group):
            columns = slice(g * query_block, (g + 1) * query_block)
            out_columns = slice(g * HEAD_SIZE, (g + 1) * HEAD_SIZE)
            tokens = numer[:, columns].T
            if not rows_each:
                numer_refs[0][rows, out_columns] = tokens
                continue
            tokens = tokens.reshape(-1, CORES, rows_each, HEAD_SIZE)
            first = lax.rem(lax.axis_index("ctx"), CORES) == 0
            half = pl.ds(at * query_block // CORES, query_block // CORES)
            kept = jnp.where(first, tokens[:, 0], tokens[:, 1]).reshape(-1, HEAD_SIZE)
            sent = jnp.where(first, tokens[:, 1], tokens[:, 0]).reshape(-1, HEAD_SIZE)
            numer_refs[0][half, out_columns] = kept
            numer_refs[1][half, out_columns] = sent.astype(jnp.bfloat16)


def attend(whole, keys, values, block_mask, rows_each):
    qtok, width = whole.shape
    kdev = keys.shape[0]
    heads_kv, query_blocks, key_blocks = block_mask.shape
    columns = width // heads_kv
    lanes = columns // HEAD_SIZE * (qtok // query_blocks)
    stat = jax.ShapeDtypeStruct((heads_kv, query_blocks, lanes), jnp.float32)
    stat_spec = pl.BlockSpec((1, query_blocks, lanes), lambda h: (h, 0, 0))
    numers = [jax.ShapeDtypeStruct((qtok, width), jnp.float32)]
    if rows_each:
        numers = [jax.ShapeDtypeStruct((qtok // CORES, width), t) for t in (jnp.float32, jnp.bfloat16)]
    return pl.pallas_call(
        functools.partial(attend_kernel, rows_each),
        grid=(heads_kv,),
        out_shape=(*numers, stat, stat),
        in_specs=[
            pl.BlockSpec(memory_space=pltpu.SMEM),
            pl.BlockSpec((qtok, columns), lambda h: (0, h)),
            pl.BlockSpec((kdev, HEAD_SIZE), lambda h: (0, h)),
            pl.BlockSpec((kdev, HEAD_SIZE), lambda h: (0, h)),
        ],
        out_specs=(
            *(pl.BlockSpec((numer.shape[0], columns), lambda h: (0, h)) for numer in numers),
            stat_spec,
            stat_spec,
        ),
        scratch_shapes=[
            pltpu.SMEM((key_blocks + 2,), jnp.int32),
            pltpu.VMEM(((key_blocks + 1) // 2, 2 * kdev // key_blocks, lanes), jnp.float32),
            pltpu.VMEM((HEAD_SIZE, lanes), jnp.bfloat16),
            pltpu.VMEM((HEAD_SIZE + ONES, kdev), jnp.bfloat16),
            pltpu.VMEM((HEAD_SIZE + ONES, lanes), jnp.float32),
        ],
        compiler_params=pltpu.CompilerParams(vmem_limit_bytes=60 * 2**20),
        name="attend",
    )(block_mask, whole, keys, values)


def by_token(stat, qtok):
    heads_kv, query_blocks, _ = stat.shape
    stat = stat.reshape(heads_kv, query_blocks, -1, qtok // query_blocks)
    return stat.transpose(1, 3, 0, 2).reshape(qtok, -1)


def shards_any(queries, keys, values, block_mask, out_weight):
    whole = lax.all_gather(queries, "ctx", axis=0, tiled=True)
    qtok, width = whole.shape
    numer, top, total = attend(whole, keys, values, block_mask, 0)
    rescale = by_token(jnp.exp2(top - lax.pmax(top, "ctx")), qtok)
    denom = by_token(total, qtok) * rescale
    numer = (numer.reshape(qtok, -1, HEAD_SIZE) * rescale[:, :, None]).reshape(qtok, width)
    num_rows = lax.psum_scatter(numer, "ctx", scatter_dimension=0, tiled=True)
    den_rows = lax.psum_scatter(denom, "ctx", scatter_dimension=0, tiled=True)
    own_rows = num_rows.shape[0]
    attn_rows = (num_rows.reshape(own_rows, -1, HEAD_SIZE) / den_rows[:, :, None]).reshape(
        own_rows, width
    )
    attn_cols = lax.all_to_all(
        attn_rows.astype(jnp.bfloat16), "ctx", split_axis=1, concat_axis=0, tiled=True
    )
    summed = lax.psum_scatter(
        jnp.dot(attn_cols, out_weight, preferred_element_type=jnp.float32),
        "ctx",
        scatter_dimension=0,
        tiled=True,
    )
    return summed.astype(jnp.bfloat16)


def place(n):
    me = lax.axis_index("ctx")
    core = lax.rem(me, CORES)
    x = lax.rem(me // CORES, ROW)
    plane = me // (CORES * ROW)
    return me, plane, x, core


def index_of(plane, x, core):
    return (plane * ROW + x) * CORES + core


def greet(devices):
    barrier = pltpu.get_barrier_semaphore()
    for device in devices:
        pl.semaphore_signal(barrier, inc=1, device_id={"ctx": device}, device_id_type=MESH)
    pl.semaphore_wait(barrier, len(devices))


def remote(src, dst, send, recv, device):
    return pltpu.make_async_remote_copy(
        src_ref=src,
        dst_ref=dst,
        send_sem=send,
        recv_sem=recv,
        device_id={"ctx": device},
        device_id_type=MESH,
    )


def gather_kernel(n, own_ref, whole_ref, own_sem, send_sem, recv_sem):
    me, plane, x, core = place(n)
    planes = n // (CORES * ROW)
    beside, sibling = 1 - x, 1 - core
    barrier = pltpu.get_barrier_semaphore()

    def hello(device):
        pl.semaphore_signal(barrier, inc=1, device_id={"ctx": device}, device_id_type=MESH)

    hello(index_of(plane, beside, core))
    hello(index_of(plane, x, sibling))

    @pl.when(plane > 0)
    def _():
        hello(index_of(plane - 1, x, core))

    @pl.when(plane < planes - 1)
    def _():
        hello(index_of(plane + 1, x, core))

    ends = (plane > 0).astype(jnp.int32) + (plane < planes - 1).astype(jnp.int32)
    pl.semaphore_wait(barrier, 2 + ends)
    own = pltpu.make_async_copy(own_ref, whole_ref.at[me], own_sem)
    own.start()

    def copy_to(block, way, device, mine=False):
        src = own_ref if mine else whole_ref.at[block]
        return remote(src, whole_ref.at[block], send_sem.at[way, block], recv_sem.at[block], device)

    def arrived(block):
        copy_to(block, 0, me).wait_recv()

    def pass_on(p, up, act, mine=False):
        block = index_of(p, x, core)

        @pl.when(plane + up < planes if up > 0 else plane + up >= 0)
        def _():
            act(copy_to(block, 0 if up > 0 else 1, index_of(plane + up, x, core), mine))

    start, ended = (lambda copy: copy.start()), (lambda copy: copy.wait_send())
    pass_on(plane, 1, start, True)
    pass_on(plane, -1, start, True)
    copy_to(me, 2, index_of(plane, beside, core), True).start()
    copy_to(me, 3, index_of(plane, x, sibling), True).start()
    for distance in range(1, planes):
        for up in (1, -1):
            p = plane - up * distance

            @pl.when(p >= 0 if up > 0 else p < planes)
            def _():
                block = index_of(p, x, core)
                arrived(block)
                pass_on(p, up, start)
                copy_to(block, 2, index_of(plane, beside, core)).start()
                copy_to(block, 3, index_of(plane, x, sibling)).start()

    def near_first(act):
        act(plane)
        for distance in range(1, planes):
            for up in (1, -1):
                p = plane - up * distance

                @pl.when(p >= 0 if up > 0 else p < planes)
                def _():
                    act(p)

    def from_beside(p):
        block = index_of(p, beside, core)
        arrived(block)
        copy_to(block, 3, index_of(plane, x, sibling)).start()

    def from_sibling(p):
        arrived(index_of(p, x, sibling))
        arrived(index_of(p, beside, sibling))

    near_first(from_beside)
    near_first(from_sibling)
    pass_on(plane, 1, ended, True)
    pass_on(plane, -1, ended, True)
    for distance in range(1, planes):
        for up in (1, -1):
            p = plane - up * distance

            @pl.when(p >= 0 if up > 0 else p < planes)
            def _():
                pass_on(p, up, ended)

    def sent(p):
        copy_to(index_of(p, x, core), 2, index_of(plane, beside, core)).wait_send()
        copy_to(index_of(p, x, core), 3, index_of(plane, x, sibling)).wait_send()
        copy_to(index_of(p, beside, core), 3, index_of(plane, x, sibling)).wait_send()

    near_first(sent)
    own.wait()


def gather_rows(queries, n):
    rows, width = queries.shape
    whole = pl.pallas_call(
        functools.partial(gather_kernel, n),
        out_shape=jax.ShapeDtypeStruct((n, rows, width), queries.dtype),
        in_specs=[pl.BlockSpec(memory_space=pltpu.VMEM)],
        out_specs=pl.BlockSpec(memory_space=pltpu.VMEM),
        scratch_shapes=[
            pltpu.SemaphoreType.DMA,
            pltpu.SemaphoreType.DMA((4, n)),
            pltpu.SemaphoreType.DMA((n,)),
        ],
        compiler_params=pltpu.CompilerParams(collective_id=0, has_side_effects=True),
        name="gather_rows",
    )(queries)
    return whole.reshape(n * rows, width)


def reduce_rows(place_of, parts, merge, finish):
    plane, x, core, planes = place_of
    beside, sibling = 1 - x, 1 - core
    others = [lax.rem(plane + step, planes) for step in range(1, planes)]

    def turn(step):
        return lax.rem(plane + 1 + step, planes)

    def core_copy(part, p):
        sem = part[9]
        return remote(
            part[0](p), part[2].at[p], sem.at[0, p], sem.at[1, p], index_of(plane, x, sibling)
        )

    def beside_copy(part, p):
        sem = part[9]
        return remote(
            part[3].at[p], part[5].at[p], sem.at[2, p], sem.at[3, p], index_of(plane, beside, core)
        )

    def plane_copy(part, p, slot):
        sem = part[9]
        return remote(
            part[6].at[p], part[8].at[slot], sem.at[4, p], sem.at[5, slot], index_of(p, x, core)
        )

    for p in others + [plane]:
        for part in parts:
            core_copy(part, p).start()

    def from_core(step, _):
        p = turn(step)
        for part in parts:
            core_copy(part, p).wait_recv()
        for side, out in ((beside, 3), (x, 4)):
            merge(
                [part[1](p, side) for part in parts],
                [part[2].at[p, side] for part in parts],
                [part[out].at[p] for part in parts],
            )
            if out == 3:
                for part in parts:
                    beside_copy(part, p).start()
        return 0

    lax.fori_loop(0, planes, from_core, 0)

    def from_beside(p, outs):
        for part in parts:
            beside_copy(part, p).wait_recv()
        merge([part[4].at[p] for part in parts], [part[5].at[p] for part in parts], outs)

    def to_plane(step, _):
        p = turn(step)
        from_beside(p, [part[6].at[p] for part in parts])
        for part in parts:
            plane_copy(part, p, plane).start()
        return 0

    lax.fori_loop(0, planes - 1, to_plane, 0)
    from_beside(plane, [part[7] for part in parts])
    for p in others:
        for part in parts:
            plane_copy(part, p, p).wait_recv()
    finish([[part[7] for part in parts]] + [[part[8].at[p] for part in parts] for p in others])
    for p in others + [plane]:
        for part in parts:
            core_copy(part, p).wait_send()
            beside_copy(part, p).wait_send()
    for p in others:
        for part in parts:
            plane_copy(part, p, plane).wait_send()


def reduce_scratch(planes, rows, width, dtype):
    return [
        pltpu.VMEM((planes, ROW, rows, width), dtype),
        pltpu.VMEM((planes, rows, width), dtype),
        pltpu.VMEM((planes, rows, width), jnp.float32),
        pltpu.VMEM((planes, rows, width), dtype),
        pltpu.VMEM((planes, rows, width), dtype),
        pltpu.VMEM((rows, width), jnp.float32),
        pltpu.VMEM((planes, rows, width), dtype),
        pltpu.SemaphoreType.DMA((6, planes)),
    ]


STATS = 128


def weigh(stats):
    half = STATS // 2
    tops = [stat[:, :half] for stat in stats]
    top = functools.reduce(jnp.maximum, tops)
    factors = [jnp.exp2(one - top) for one in tops]
    total = sum(stat[:, half:] * factor for stat, factor in zip(stats, factors))
    return top, factors, total


def combine_kernel(n, kept_hbm, sent_ref, stat_ref, cols_ref, *scratch):
    numer_scratch, stat_scratch = scratch[:8], scratch[8:16]
    piece_ref, swap_send, swap_recv, own_sem, kept_ref, kept_sem = scratch[16:]
    keep = pltpu.make_async_copy(kept_hbm, kept_ref, kept_sem)
    keep.start()
    me, plane, x, core = place(n)
    planes = n // (CORES * ROW)
    width = kept_ref.shape[-1]
    heads = width // HEAD_SIZE
    others = [lax.rem(me + step, n) for step in range(1, n)]
    greet(others)
    keep.wait()

    def merge(one, two, out):
        top, factors, total = weigh([one[1][...], two[1][...]])
        out[1][...] = jnp.concatenate([top, total], axis=1)
        for head in range(heads):
            at = slice(head * HEAD_SIZE, (head + 1) * HEAD_SIZE)
            out[0][:, at] = (
                one[0][:, at].astype(jnp.float32) * factors[0][:, head : head + 1]
                + two[0][:, at].astype(jnp.float32) * factors[1][:, head : head + 1]
            ).astype(out[0].dtype)

    def finish(sources):
        _, factors, total = weigh([source[1][...] for source in sources])
        out = []
        for head in range(heads):
            at = slice(head * HEAD_SIZE, (head + 1) * HEAD_SIZE)
            numer = sum(
                source[0][:, at].astype(jnp.float32) * factor[:, head : head + 1]
                for source, factor in zip(sources, factors)
            )
            out.append((numer / total[:, head : head + 1]).astype(jnp.bfloat16))
        attn = jnp.concatenate(out, axis=1)
        share = width // n
        for device in range(n):
            piece_ref[device] = attn[:, device * share : (device + 1) * share]

    reduce_rows(
        (plane, x, core, planes),
        [
            (lambda p: sent_ref.at[p], lambda p, side: kept_ref.at[p, side], *numer_scratch),
            (
                lambda p: stat_ref.at[p, :, 1 - core],
                lambda p, side: stat_ref.at[p, side, core],
                *stat_scratch,
            ),
        ],
        merge,
        finish,
    )

    def swap(device, slot):
        return remote(
            piece_ref.at[device], cols_ref.at[slot], swap_send.at[device], swap_recv.at[slot], device
        )

    own = pltpu.make_async_copy(piece_ref.at[me], cols_ref.at[me], own_sem)
    own.start()
    for device in others:
        swap(device, me).start()
    own.wait()
    for device in others:
        swap(device, device).wait_recv()
    for device in others:
        swap(device, me).wait_send()


def combine(kept, sent, stats, n):
    qtok, width = stats.shape[0], kept.shape[1]
    planes, rows = n // (CORES * ROW), qtok // n
    cols = pl.pallas_call(
        functools.partial(combine_kernel, n),
        out_shape=jax.ShapeDtypeStruct((n, rows, width // n), jnp.bfloat16),
        in_specs=[pl.BlockSpec(memory_space=pl.ANY)] * 2
        + [pl.BlockSpec(memory_space=pltpu.VMEM)],
        out_specs=pl.BlockSpec(memory_space=pltpu.VMEM),
        scratch_shapes=reduce_scratch(planes, rows, width, jnp.bfloat16)
        + reduce_scratch(planes, rows, STATS, jnp.float32)
        + [
            pltpu.VMEM((n, rows, width // n), jnp.bfloat16),
            pltpu.SemaphoreType.DMA((n,)),
            pltpu.SemaphoreType.DMA((n,)),
            pltpu.SemaphoreType.DMA,
            pltpu.VMEM((planes, ROW, rows, width), jnp.float32),
            pltpu.SemaphoreType.DMA,
        ],
        compiler_params=pltpu.CompilerParams(
            collective_id=1, has_side_effects=True, vmem_limit_bytes=60 * 2**20
        ),
        name="combine",
    )(
        kept.reshape(planes, ROW, rows, width),
        sent.reshape(planes, ROW, rows, width),
        stats.reshape(planes, ROW, CORES, rows, STATS),
    )
    return cols.reshape(qtok, width // n)


TILE = 512


def project_kernel(n, cols_ref, weight_hbm, out_ref, weight_ref, weight_sem, kept_ref, sent_ref, *scratch):
    _, plane, x, core = place(n)
    planes = n // (CORES * ROW)
    rows, width = out_ref.shape

    def fetch(tile):
        at = pl.ds(pl.multiple_of(tile * TILE, TILE), TILE)
        return pltpu.make_async_copy(weight_hbm.at[:, at], weight_ref.at[:, at], weight_sem.at[tile])

    for tile in range(width // TILE):
        fetch(tile).start()
    greet(
        [index_of(lax.rem(plane + step, planes), x, core) for step in range(1, planes)]
        + [index_of(plane, 1 - x, core), index_of(plane, x, 1 - core)]
    )

    def tile_step(tile, _):
        at = pl.ds(pl.multiple_of(tile * TILE, TILE), TILE)
        fetch(tile).wait()
        product = jnp.dot(cols_ref[...], weight_ref[:, at], preferred_element_type=jnp.float32)
        product = product.reshape(planes, ROW, CORES, rows, TILE)
        kept_ref[:, :, :, at] = jnp.where(core == 0, product[:, :, 0], product[:, :, 1])
        sent = jnp.where(core == 0, product[:, :, 1], product[:, :, 0])
        sent_ref[:, :, :, at] = sent.astype(sent_ref.dtype)
        return 0

    lax.fori_loop(0, width // TILE, tile_step, 0)

    def merge(one, two, out):
        out[0][...] = (one[0][...].astype(jnp.float32) + two[0][...].astype(jnp.float32)).astype(
            out[0].dtype
        )

    def finish(sources):
        out_ref[...] = sum(source[0][...].astype(jnp.float32) for source in sources).astype(
            out_ref.dtype
        )

    reduce_rows((plane, x, core, planes), [(lambda p: sent_ref.at[p], lambda p, side: kept_ref.at[p, side], *scratch)], merge, finish)


def project(cols, weight, n):
    qtok = cols.shape[0]
    width = weight.shape[1]
    planes, rows = n // (CORES * ROW), qtok // n
    return pl.pallas_call(
        functools.partial(project_kernel, n),
        out_shape=jax.ShapeDtypeStruct((rows, width), jnp.bfloat16),
        in_specs=[pl.BlockSpec(memory_space=pltpu.VMEM), pl.BlockSpec(memory_space=pl.ANY)],
        out_specs=pl.BlockSpec(memory_space=pltpu.VMEM),
        scratch_shapes=[
            pltpu.VMEM(weight.shape, weight.dtype),
            pltpu.SemaphoreType.DMA((width // TILE,)),
        ]
        + [pltpu.VMEM((planes, ROW, rows, width), t) for t in (jnp.float32, jnp.bfloat16)]
        + reduce_scratch(planes, rows, width, jnp.bfloat16),
        compiler_params=pltpu.CompilerParams(
            collective_id=2, has_side_effects=True, vmem_limit_bytes=60 * 2**20
        ),
        name="project",
    )(cols, weight)


def shards_near(n, queries, keys, values, block_mask, out_weight):
    whole = gather_rows(queries, n)
    qtok = whole.shape[0]
    kept, sent, top, total = attend(whole, keys, values, block_mask, queries.shape[0])
    top, total = by_token(top, qtok), by_token(total, qtok)
    room = ((0, 0), (0, STATS // 2 - top.shape[1]))
    stats = jnp.concatenate([jnp.pad(top, room), jnp.pad(total, room)], axis=1)
    cols = combine(kept, sent, stats, n)
    return project(cols, out_weight, n)


def solution(mesh):
    n = mesh.shape["ctx"]

    def shards(queries, *rest):
        fits = n % (CORES * ROW) == 0 and queries.shape[0] == 16
        if fits and queries.shape[1] // HEAD_SIZE <= STATS // 2:
            return shards_near(n, queries, *rest)
        return shards_any(queries, *rest)

    return jax.shard_map(
        shards,
        mesh=mesh,
        in_specs=(
            P(("groups", "ctx"), None),
            P(("groups", "ctx"), None),
            P(("groups", "ctx"), None),
            P("groups", None, "ctx"),
            P("ctx", None),
        ),
        out_specs=P(("groups", "ctx"), None),
        check_vma=False,
    )
```

```python
import functools
import math

import jax
import jax.numpy as jnp
from jax import lax
from jax.experimental import pallas as pl
from jax.experimental.pallas import tpu as pltpu
from jax.sharding import PartitionSpec as P

HEAD_SIZE = 128
NEG = -1e30
ONES = 16
LOG2E = math.log2(math.e)
MESH = pl.DeviceIdType.MESH
CORES, ROW = 2, 2


def attend_kernel(rows_each, mask_ref, q_ref, k_ref, v_ref, *refs):
    *numer_refs, top_ref, total_ref, live_ref, score_ref, query_ref, value_ref, sum_ref = refs
    head = pl.program_id(0)
    query_blocks, key_blocks = mask_ref.shape[1:]
    key_block = k_ref.shape[0] // key_blocks
    query_block = q_ref.shape[0] // query_blocks
    group = q_ref.shape[1] // HEAD_SIZE
    factor = LOG2E / math.sqrt(HEAD_SIZE)
    value_ref[:HEAD_SIZE] = v_ref[...].T
    value_ref[HEAD_SIZE:] = jnp.ones((ONES, v_ref.shape[0]), jnp.bfloat16)
    for at in range(query_blocks):
        rows = pl.ds(at * query_block, query_block)
        count = jnp.int32(0)
        for block in range(key_blocks):
            live_ref[count] = block
            count = count + (mask_ref[head, at, block] > 0).astype(jnp.int32)
        live_ref[count] = 0
        for g in range(group):
            tokens = q_ref[rows, g * HEAD_SIZE : (g + 1) * HEAD_SIZE]
            query_ref[:, g * query_block : (g + 1) * query_block] = tokens.T
        lanes = query_ref.shape[1]
        pairs = (count + 1) // 2

        def start_of(which):
            return pl.multiple_of(live_ref[which] * key_block, key_block)

        eights, quads = (count + 1) // 8, (count + 1) // 4

        def taken(ref_slice, first, blocks, axis):
            return jnp.concatenate([ref_slice(start_of(first + b)) for b in range(blocks)], axis=axis)

        def score_step(blocks, step, top):
            pair = step * (blocks // 2)
            keys = taken(lambda at: k_ref[pl.ds(at, key_block), :], 2 * pair, blocks, 0)
            scores = jnp.dot(keys, query_ref[...], preferred_element_type=jnp.float32)
            score_ref[pl.ds(pair, blocks // 2)] = scores.reshape(blocks // 2, 2 * key_block, lanes)
            tops = jnp.max(scores.reshape(blocks, key_block // 8, 8, lanes), axis=1)
            for b in range(blocks):
                one = tops[b]
                if b == blocks - 1:
                    one = jnp.where(2 * pair + b < count, one, NEG)
                top = jnp.maximum(top, one)
            return top

        top = jnp.full((8, lanes), NEG, jnp.float32)
        top = lax.fori_loop(0, eights, functools.partial(score_step, 8), top)
        top = lax.fori_loop(2 * eights, quads, functools.partial(score_step, 4), top)
        top = lax.fori_loop(2 * quads, pairs, functools.partial(score_step, 2), top)
        top = jnp.max(top, axis=0, keepdims=True) * factor
        sum_ref[...] = jnp.zeros_like(sum_ref)

        def sum_step(blocks, step, _):
            pair = step * (blocks // 2)
            probs = []
            for b in range(blocks):
                shift = top
                if b == blocks - 1:
                    shift = jnp.where(2 * pair + b < count, top, -NEG)
                half = slice(b % 2 * key_block, (b % 2 + 1) * key_block)
                scores = score_ref[pair + b // 2, half]
                probs.append(jnp.exp2(scores * factor - shift).astype(jnp.bfloat16))
            values = taken(lambda at: value_ref[:, pl.ds(at, key_block)], 2 * pair, blocks, 1)
            sum_ref[...] += jnp.dot(
                values, jnp.concatenate(probs, axis=0), preferred_element_type=jnp.float32
            )
            return 0

        lax.fori_loop(0, eights, functools.partial(sum_step, 8), 0)
        lax.fori_loop(2 * eights, quads, functools.partial(sum_step, 4), 0)
        lax.fori_loop(2 * quads, pairs, functools.partial(sum_step, 2), 0)
        numer = sum_ref[:HEAD_SIZE]
        top_ref[0, at : at + 1, :] = top
        total_ref[0, at : at + 1, :] = sum_ref[HEAD_SIZE : HEAD_SIZE + 1]
        for g in range(group):
            columns = slice(g * query_block, (g + 1) * query_block)
            out_columns = slice(g * HEAD_SIZE, (g + 1) * HEAD_SIZE)
            tokens = numer[:, columns].T
            if not rows_each:
                numer_refs[0][rows, out_columns] = tokens
                continue
            tokens = tokens.reshape(-1, CORES, rows_each, HEAD_SIZE)
            first = lax.rem(lax.axis_index("ctx"), CORES) == 0
            half = pl.ds(at * query_block // CORES, query_block // CORES)
            kept = jnp.where(first, tokens[:, 0], tokens[:, 1]).reshape(-1, HEAD_SIZE)
            sent = jnp.where(first, tokens[:, 1], tokens[:, 0]).reshape(-1, HEAD_SIZE)
            numer_refs[0][half, out_columns] = kept
            numer_refs[1][half, out_columns] = sent.astype(jnp.bfloat16)


def attend(whole, keys, values, block_mask, rows_each):
    qtok, width = whole.shape
    kdev = keys.shape[0]
    heads_kv, query_blocks, key_blocks = block_mask.shape
    columns = width // heads_kv
    lanes = columns // HEAD_SIZE * (qtok // query_blocks)
    stat = jax.ShapeDtypeStruct((heads_kv, query_blocks, lanes), jnp.float32)
    stat_spec = pl.BlockSpec((1, query_blocks, lanes), lambda h: (h, 0, 0))
    numers = [jax.ShapeDtypeStruct((qtok, width), jnp.float32)]
    if rows_each:
        numers = [jax.ShapeDtypeStruct((qtok // CORES, width), t) for t in (jnp.float32, jnp.bfloat16)]
    return pl.pallas_call(
        functools.partial(attend_kernel, rows_each),
        grid=(heads_kv,),
        out_shape=(*numers, stat, stat),
        in_specs=[
            pl.BlockSpec(memory_space=pltpu.SMEM),
            pl.BlockSpec((qtok, columns), lambda h: (0, h)),
            pl.BlockSpec((kdev, HEAD_SIZE), lambda h: (0, h)),
            pl.BlockSpec((kdev, HEAD_SIZE), lambda h: (0, h)),
        ],
        out_specs=(
            *(pl.BlockSpec((numer.shape[0], columns), lambda h: (0, h)) for numer in numers),
            stat_spec,
            stat_spec,
        ),
        scratch_shapes=[
            pltpu.SMEM((key_blocks + 2,), jnp.int32),
            pltpu.VMEM(((key_blocks + 1) // 2, 2 * kdev // key_blocks, lanes), jnp.float32),
            pltpu.VMEM((HEAD_SIZE, lanes), jnp.bfloat16),
            pltpu.VMEM((HEAD_SIZE + ONES, kdev), jnp.bfloat16),
            pltpu.VMEM((HEAD_SIZE + ONES, lanes), jnp.float32),
        ],
        compiler_params=pltpu.CompilerParams(vmem_limit_bytes=60 * 2**20),
        name="attend",
    )(block_mask, whole, keys, values)


def by_token(stat, qtok):
    heads_kv, query_blocks, _ = stat.shape
    stat = stat.reshape(heads_kv, query_blocks, -1, qtok // query_blocks)
    return stat.transpose(1, 3, 0, 2).reshape(qtok, -1)


def shards_any(queries, keys, values, block_mask, out_weight):
    whole = lax.all_gather(queries, "ctx", axis=0, tiled=True)
    qtok, width = whole.shape
    numer, top, total = attend(whole, keys, values, block_mask, 0)
    rescale = by_token(jnp.exp2(top - lax.pmax(top, "ctx")), qtok)
    denom = by_token(total, qtok) * rescale
    numer = (numer.reshape(qtok, -1, HEAD_SIZE) * rescale[:, :, None]).reshape(qtok, width)
    num_rows = lax.psum_scatter(numer, "ctx", scatter_dimension=0, tiled=True)
    den_rows = lax.psum_scatter(denom, "ctx", scatter_dimension=0, tiled=True)
    own_rows = num_rows.shape[0]
    attn_rows = (num_rows.reshape(own_rows, -1, HEAD_SIZE) / den_rows[:, :, None]).reshape(
        own_rows, width
    )
    attn_cols = lax.all_to_all(
        attn_rows.astype(jnp.bfloat16), "ctx", split_axis=1, concat_axis=0, tiled=True
    )
    summed = lax.psum_scatter(
        jnp.dot(attn_cols, out_weight, preferred_element_type=jnp.float32),
        "ctx",
        scatter_dimension=0,
        tiled=True,
    )
    return summed.astype(jnp.bfloat16)


def place(n):
    me = lax.axis_index("ctx")
    core = lax.rem(me, CORES)
    x = lax.rem(me // CORES, ROW)
    plane = me // (CORES * ROW)
    return me, plane, x, core


def index_of(plane, x, core):
    return (plane * ROW + x) * CORES + core


def greet(devices):
    barrier = pltpu.get_barrier_semaphore()
    for device in devices:
        pl.semaphore_signal(barrier, inc=1, device_id={"ctx": device}, device_id_type=MESH)
    pl.semaphore_wait(barrier, len(devices))


def remote(src, dst, send, recv, device):
    return pltpu.make_async_remote_copy(
        src_ref=src,
        dst_ref=dst,
        send_sem=send,
        recv_sem=recv,
        device_id={"ctx": device},
        device_id_type=MESH,
    )


def gather_kernel(n, own_ref, whole_ref, own_sem, send_sem, recv_sem):
    me, plane, x, core = place(n)
    planes = n // (CORES * ROW)
    beside, sibling = 1 - x, 1 - core
    barrier = pltpu.get_barrier_semaphore()

    def hello(device):
        pl.semaphore_signal(barrier, inc=1, device_id={"ctx": device}, device_id_type=MESH)

    hello(index_of(plane, beside, core))
    hello(index_of(plane, x, sibling))

    @pl.when(plane > 0)
    def _():
        hello(index_of(plane - 1, x, core))

    @pl.when(plane < planes - 1)
    def _():
        hello(index_of(plane + 1, x, core))

    ends = (plane > 0).astype(jnp.int32) + (plane < planes - 1).astype(jnp.int32)
    pl.semaphore_wait(barrier, 2 + ends)
    own = pltpu.make_async_copy(own_ref, whole_ref.at[me], own_sem)
    own.start()

    def copy_to(block, way, device, mine=False):
        src = own_ref if mine else whole_ref.at[block]
        return remote(src, whole_ref.at[block], send_sem.at[way, block], recv_sem.at[block], device)

    def arrived(block):
        copy_to(block, 0, me).wait_recv()

    def pass_on(p, up, act, mine=False):
        block = index_of(p, x, core)

        @pl.when(plane + up < planes if up > 0 else plane + up >= 0)
        def _():
            act(copy_to(block, 0 if up > 0 else 1, index_of(plane + up, x, core), mine))

    start, ended = (lambda copy: copy.start()), (lambda copy: copy.wait_send())
    pass_on(plane, 1, start, True)
    pass_on(plane, -1, start, True)
    copy_to(me, 2, index_of(plane, beside, core), True).start()
    copy_to(me, 3, index_of(plane, x, sibling), True).start()
    for distance in range(1, planes):
        for up in (1, -1):
            p = plane - up * distance

            @pl.when(p >= 0 if up > 0 else p < planes)
            def _():
                block = index_of(p, x, core)
                arrived(block)
                pass_on(p, up, start)
                copy_to(block, 2, index_of(plane, beside, core)).start()
                copy_to(block, 3, index_of(plane, x, sibling)).start()

    def near_first(act):
        act(plane)
        for distance in range(1, planes):
            for up in (1, -1):
                p = plane - up * distance

                @pl.when(p >= 0 if up > 0 else p < planes)
                def _():
                    act(p)

    def from_beside(p):
        block = index_of(p, beside, core)
        arrived(block)
        copy_to(block, 3, index_of(plane, x, sibling)).start()

    def from_sibling(p):
        arrived(index_of(p, x, sibling))
        arrived(index_of(p, beside, sibling))

    near_first(from_beside)
    near_first(from_sibling)
    pass_on(plane, 1, ended, True)
    pass_on(plane, -1, ended, True)
    for distance in range(1, planes):
        for up in (1, -1):
            p = plane - up * distance

            @pl.when(p >= 0 if up > 0 else p < planes)
            def _():
                pass_on(p, up, ended)

    def sent(p):
        copy_to(index_of(p, x, core), 2, index_of(plane, beside, core)).wait_send()
        copy_to(index_of(p, x, core), 3, index_of(plane, x, sibling)).wait_send()
        copy_to(index_of(p, beside, core), 3, index_of(plane, x, sibling)).wait_send()

    near_first(sent)
    own.wait()


def gather_rows(queries, n):
    rows, width = queries.shape
    whole = pl.pallas_call(
        functools.partial(gather_kernel, n),
        out_shape=jax.ShapeDtypeStruct((n, rows, width), queries.dtype),
        in_specs=[pl.BlockSpec(memory_space=pltpu.VMEM)],
        out_specs=pl.BlockSpec(memory_space=pltpu.VMEM),
        scratch_shapes=[
            pltpu.SemaphoreType.DMA,
            pltpu.SemaphoreType.DMA((4, n)),
            pltpu.SemaphoreType.DMA((n,)),
        ],
        compiler_params=pltpu.CompilerParams(collective_id=0, has_side_effects=True),
        name="gather_rows",
    )(queries)
    return whole.reshape(n * rows, width)


def reduce_rows(place_of, parts, merge, finish):
    plane, x, core, planes = place_of
    beside, sibling = 1 - x, 1 - core
    others = [lax.rem(plane + step, planes) for step in range(1, planes)]

    def turn(step):
        return lax.rem(plane + 1 + step, planes)

    def core_copy(part, p):
        sem = part[9]
        return remote(
            part[0](p), part[2].at[p], sem.at[0, p], sem.at[1, p], index_of(plane, x, sibling)
        )

    def beside_copy(part, p):
        sem = part[9]
        return remote(
            part[3].at[p], part[5].at[p], sem.at[2, p], sem.at[3, p], index_of(plane, beside, core)
        )

    def plane_copy(part, p, slot):
        sem = part[9]
        return remote(
            part[6].at[p], part[8].at[slot], sem.at[4, p], sem.at[5, slot], index_of(p, x, core)
        )

    for p in others + [plane]:
        for part in parts:
            core_copy(part, p).start()

    def from_core(step, _):
        p = turn(step)
        for part in parts:
            core_copy(part, p).wait_recv()
        for side, out in ((beside, 3), (x, 4)):
            merge(
                [part[1](p, side) for part in parts],
                [part[2].at[p, side] for part in parts],
                [part[out].at[p] for part in parts],
            )
            if out == 3:
                for part in parts:
                    beside_copy(part, p).start()
        return 0

    lax.fori_loop(0, planes, from_core, 0)

    def from_beside(p, outs):
        for part in parts:
            beside_copy(part, p).wait_recv()
        merge([part[4].at[p] for part in parts], [part[5].at[p] for part in parts], outs)

    def to_plane(step, _):
        p = turn(step)
        from_beside(p, [part[6].at[p] for part in parts])
        for part in parts:
            plane_copy(part, p, plane).start()
        return 0

    lax.fori_loop(0, planes - 1, to_plane, 0)
    from_beside(plane, [part[7] for part in parts])
    for p in others:
        for part in parts:
            plane_copy(part, p, p).wait_recv()
    finish([[part[7] for part in parts]] + [[part[8].at[p] for part in parts] for p in others])
    for p in others + [plane]:
        for part in parts:
            core_copy(part, p).wait_send()
            beside_copy(part, p).wait_send()
    for p in others:
        for part in parts:
            plane_copy(part, p, plane).wait_send()


def reduce_scratch(planes, rows, width, dtype):
    return [
        pltpu.VMEM((planes, ROW, rows, width), dtype),
        pltpu.VMEM((planes, rows, width), dtype),
        pltpu.VMEM((planes, rows, width), jnp.float32),
        pltpu.VMEM((planes, rows, width), dtype),
        pltpu.VMEM((planes, rows, width), dtype),
        pltpu.VMEM((rows, width), jnp.float32),
        pltpu.VMEM((planes, rows, width), dtype),
        pltpu.SemaphoreType.DMA((6, planes)),
    ]


STATS = 128


def weigh(stats):
    half = STATS // 2
    tops = [stat[:, :half] for stat in stats]
    top = functools.reduce(jnp.maximum, tops)
    factors = [jnp.exp2(one - top) for one in tops]
    total = sum(stat[:, half:] * factor for stat, factor in zip(stats, factors))
    return top, factors, total


def combine_kernel(n, kept_hbm, sent_ref, stat_ref, cols_ref, *scratch):
    numer_scratch, stat_scratch = scratch[:8], scratch[8:16]
    piece_ref, swap_send, swap_recv, own_sem, kept_ref, kept_sem = scratch[16:]
    keep = pltpu.make_async_copy(kept_hbm, kept_ref, kept_sem)
    keep.start()
    me, plane, x, core = place(n)
    planes = n // (CORES * ROW)
    width = kept_ref.shape[-1]
    heads = width // HEAD_SIZE
    others = [lax.rem(me + step, n) for step in range(1, n)]
    greet(others)
    keep.wait()

    def merge(one, two, out):
        top, factors, total = weigh([one[1][...], two[1][...]])
        out[1][...] = jnp.concatenate([top, total], axis=1)
        for head in range(heads):
            at = slice(head * HEAD_SIZE, (head + 1) * HEAD_SIZE)
            out[0][:, at] = (
                one[0][:, at].astype(jnp.float32) * factors[0][:, head : head + 1]
                + two[0][:, at].astype(jnp.float32) * factors[1][:, head : head + 1]
            ).astype(out[0].dtype)

    def finish(sources):
        _, factors, total = weigh([source[1][...] for source in sources])
        out = []
        for head in range(heads):
            at = slice(head * HEAD_SIZE, (head + 1) * HEAD_SIZE)
            numer = sum(
                source[0][:, at].astype(jnp.float32) * factor[:, head : head + 1]
                for source, factor in zip(sources, factors)
            )
            out.append((numer / total[:, head : head + 1]).astype(jnp.bfloat16))
        attn = jnp.concatenate(out, axis=1)
        share = width // n
        for device in range(n):
            piece_ref[device] = attn[:, device * share : (device + 1) * share]

    reduce_rows(
        (plane, x, core, planes),
        [
            (lambda p: sent_ref.at[p], lambda p, side: kept_ref.at[p, side], *numer_scratch),
            (
                lambda p: stat_ref.at[p, :, 1 - core],
                lambda p, side: stat_ref.at[p, side, core],
                *stat_scratch,
            ),
        ],
        merge,
        finish,
    )

    def swap(device, slot):
        return remote(
            piece_ref.at[device], cols_ref.at[slot], swap_send.at[device], swap_recv.at[slot], device
        )

    own = pltpu.make_async_copy(piece_ref.at[me], cols_ref.at[me], own_sem)
    own.start()
    for device in others:
        swap(device, me).start()
    own.wait()
    for device in others:
        swap(device, device).wait_recv()
    for device in others:
        swap(device, me).wait_send()


def combine(kept, sent, stats, n):
    qtok, width = stats.shape[0], kept.shape[1]
    planes, rows = n // (CORES * ROW), qtok // n
    cols = pl.pallas_call(
        functools.partial(combine_kernel, n),
        out_shape=jax.ShapeDtypeStruct((n, rows, width // n), jnp.bfloat16),
        in_specs=[pl.BlockSpec(memory_space=pl.ANY)] * 2
        + [pl.BlockSpec(memory_space=pltpu.VMEM)],
        out_specs=pl.BlockSpec(memory_space=pltpu.VMEM),
        scratch_shapes=reduce_scratch(planes, rows, width, jnp.bfloat16)
        + reduce_scratch(planes, rows, STATS, jnp.float32)
        + [
            pltpu.VMEM((n, rows, width // n), jnp.bfloat16),
            pltpu.SemaphoreType.DMA((n,)),
            pltpu.SemaphoreType.DMA((n,)),
            pltpu.SemaphoreType.DMA,
            pltpu.VMEM((planes, ROW, rows, width), jnp.float32),
            pltpu.SemaphoreType.DMA,
        ],
        compiler_params=pltpu.CompilerParams(
            collective_id=1, has_side_effects=True, vmem_limit_bytes=60 * 2**20
        ),
        name="combine",
    )(
        kept.reshape(planes, ROW, rows, width),
        sent.reshape(planes, ROW, rows, width),
        stats.reshape(planes, ROW, CORES, rows, STATS),
    )
    return cols.reshape(qtok, width // n)


TILE = 512


def project_kernel(n, cols_ref, weight_hbm, out_ref, weight_ref, weight_sem, kept_ref, sent_ref, *scratch):
    _, plane, x, core = place(n)
    planes = n // (CORES * ROW)
    rows, width = out_ref.shape

    def fetch(tile):
        at = pl.ds(pl.multiple_of(tile * TILE, TILE), TILE)
        return pltpu.make_async_copy(weight_hbm.at[:, at], weight_ref.at[:, at], weight_sem.at[tile])

    for tile in range(width // TILE):
        fetch(tile).start()
    greet(
        [index_of(lax.rem(plane + step, planes), x, core) for step in range(1, planes)]
        + [index_of(plane, 1 - x, core), index_of(plane, x, 1 - core)]
    )

    def tile_step(tile, _):
        at = pl.ds(pl.multiple_of(tile * TILE, TILE), TILE)
        fetch(tile).wait()
        product = jnp.dot(cols_ref[...], weight_ref[:, at], preferred_element_type=jnp.float32)
        product = product.reshape(planes, ROW, CORES, rows, TILE)
        kept_ref[:, :, :, at] = jnp.where(core == 0, product[:, :, 0], product[:, :, 1])
        sent = jnp.where(core == 0, product[:, :, 1], product[:, :, 0])
        sent_ref[:, :, :, at] = sent.astype(sent_ref.dtype)
        return 0

    lax.fori_loop(0, width // TILE, tile_step, 0)

    def merge(one, two, out):
        out[0][...] = (one[0][...].astype(jnp.float32) + two[0][...].astype(jnp.float32)).astype(
            out[0].dtype
        )

    def finish(sources):
        out_ref[...] = sum(source[0][...].astype(jnp.float32) for source in sources).astype(
            out_ref.dtype
        )

    reduce_rows((plane, x, core, planes), [(lambda p: sent_ref.at[p], lambda p, side: kept_ref.at[p, side], *scratch)], merge, finish)


def project(cols, weight, n):
    qtok = cols.shape[0]
    width = weight.shape[1]
    planes, rows = n // (CORES * ROW), qtok // n
    return pl.pallas_call(
        functools.partial(project_kernel, n),
        out_shape=jax.ShapeDtypeStruct((rows, width), jnp.bfloat16),
        in_specs=[pl.BlockSpec(memory_space=pltpu.VMEM), pl.BlockSpec(memory_space=pl.ANY)],
        out_specs=pl.BlockSpec(memory_space=pltpu.VMEM),
        scratch_shapes=[
            pltpu.VMEM(weight.shape, weight.dtype),
            pltpu.SemaphoreType.DMA((width // TILE,)),
        ]
        + [pltpu.VMEM((planes, ROW, rows, width), t) for t in (jnp.float32, jnp.bfloat16)]
        + reduce_scratch(planes, rows, width, jnp.bfloat16),
        compiler_params=pltpu.CompilerParams(
            collective_id=2, has_side_effects=True, vmem_limit_bytes=60 * 2**20
        ),
        name="project",
    )(cols, weight)


def shards_near(n, queries, keys, values, block_mask, out_weight):
    whole = gather_rows(queries, n)
    qtok = whole.shape[0]
    kept, sent, top, total = attend(whole, keys, values, block_mask, queries.shape[0])
    top, total = by_token(top, qtok), by_token(total, qtok)
    room = ((0, 0), (0, STATS // 2 - top.shape[1]))
    stats = jnp.concatenate([jnp.pad(top, room), jnp.pad(total, room)], axis=1)
    cols = combine(kept, sent, stats, n)
    return project(cols, out_weight, n)


def solution(mesh):
    n = mesh.shape["ctx"]

    def shards(queries, *rest):
        fits = n % (CORES * ROW) == 0 and queries.shape[0] == 16
        if fits and queries.shape[1] // HEAD_SIZE <= STATS // 2:
            return shards_near(n, queries, *rest)
        return shards_any(queries, *rest)

    return jax.shard_map(
        shards,
        mesh=mesh,
        in_specs=(
            P(("groups", "ctx"), None),
            P(("groups", "ctx"), None),
            P(("groups", "ctx"), None),
            P("groups", None, "ctx"),
            P("ctx", None),
        ),
        out_specs=P(("groups", "ctx"), None),
        check_vma=False,
    )
```

```python
import functools
import math

import jax
import jax.numpy as jnp
from jax import lax
from jax.experimental import pallas as pl
from jax.experimental.pallas import tpu as pltpu
from jax.sharding import PartitionSpec as P

HEAD_SIZE = 128
NEG = -1e30
ONES = 16
LOG2E = math.log2(math.e)
MESH = pl.DeviceIdType.MESH
CORES, ROW = 2, 2


def attend_kernel(rows_each, mask_ref, q_ref, k_ref, v_ref, *refs):
    *numer_refs, top_ref, total_ref, live_ref, score_ref, query_ref, value_ref, sum_ref = refs
    head = pl.program_id(0)
    query_blocks, key_blocks = mask_ref.shape[1:]
    key_block = k_ref.shape[0] // key_blocks
    query_block = q_ref.shape[0] // query_blocks
    group = q_ref.shape[1] // HEAD_SIZE
    factor = LOG2E / math.sqrt(HEAD_SIZE)
    value_ref[:HEAD_SIZE] = v_ref[...].T
    value_ref[HEAD_SIZE:] = jnp.ones((ONES, v_ref.shape[0]), jnp.bfloat16)
    for at in range(query_blocks):
        rows = pl.ds(at * query_block, query_block)
        count = jnp.int32(0)
        for block in range(key_blocks):
            live_ref[count] = block
            count = count + (mask_ref[head, at, block] > 0).astype(jnp.int32)
        live_ref[count] = 0
        for g in range(group):
            tokens = q_ref[rows, g * HEAD_SIZE : (g + 1) * HEAD_SIZE]
            query_ref[:, g * query_block : (g + 1) * query_block] = tokens.T
        lanes = query_ref.shape[1]
        pairs = (count + 1) // 2

        def start_of(which):
            return pl.multiple_of(live_ref[which] * key_block, key_block)

        eights, quads = (count + 1) // 8, (count + 1) // 4

        def taken(ref_slice, first, blocks, axis):
            return jnp.concatenate([ref_slice(start_of(first + b)) for b in range(blocks)], axis=axis)

        def score_step(blocks, step, top):
            pair = step * (blocks // 2)
            keys = taken(lambda at: k_ref[pl.ds(at, key_block), :], 2 * pair, blocks, 0)
            scores = jnp.dot(keys, query_ref[...], preferred_element_type=jnp.float32)
            score_ref[pl.ds(pair, blocks // 2)] = scores.reshape(blocks // 2, 2 * key_block, lanes)
            tops = jnp.max(scores.reshape(blocks, key_block // 8, 8, lanes), axis=1)
            for b in range(blocks):
                one = tops[b]
                if b == blocks - 1:
                    one = jnp.where(2 * pair + b < count, one, NEG)
                top = jnp.maximum(top, one)
            return top

        top = jnp.full((8, lanes), NEG, jnp.float32)
        top = lax.fori_loop(0, eights, functools.partial(score_step, 8), top)
        top = lax.fori_loop(2 * eights, quads, functools.partial(score_step, 4), top)
        top = lax.fori_loop(2 * quads, pairs, functools.partial(score_step, 2), top)
        top = jnp.max(top, axis=0, keepdims=True) * factor
        sum_ref[...] = jnp.zeros_like(sum_ref)

        def sum_step(blocks, step, _):
            pair = step * (blocks // 2)
            probs = []
            for b in range(blocks):
                shift = top
                if b == blocks - 1:
                    shift = jnp.where(2 * pair + b < count, top, -NEG)
                half = slice(b % 2 * key_block, (b % 2 + 1) * key_block)
                scores = score_ref[pair + b // 2, half]
                probs.append(jnp.exp2(scores * factor - shift).astype(jnp.bfloat16))
            values = taken(lambda at: value_ref[:, pl.ds(at, key_block)], 2 * pair, blocks, 1)
            sum_ref[...] += jnp.dot(
                values, jnp.concatenate(probs, axis=0), preferred_element_type=jnp.float32
            )
            return 0

        lax.fori_loop(0, eights, functools.partial(sum_step, 8), 0)
        lax.fori_loop(2 * eights, quads, functools.partial(sum_step, 4), 0)
        lax.fori_loop(2 * quads, pairs, functools.partial(sum_step, 2), 0)
        numer = sum_ref[:HEAD_SIZE]
        top_ref[0, at : at + 1, :] = top
        total_ref[0, at : at + 1, :] = sum_ref[HEAD_SIZE : HEAD_SIZE + 1]
        for g in range(group):
            columns = slice(g * query_block, (g + 1) * query_block)
            out_columns = slice(g * HEAD_SIZE, (g + 1) * HEAD_SIZE)
            tokens = numer[:, columns].T
            if not rows_each:
                numer_refs[0][rows, out_columns] = tokens
                continue
            tokens = tokens.reshape(-1, CORES, rows_each, HEAD_SIZE)
            first = lax.rem(lax.axis_index("ctx"), CORES) == 0
            half = pl.ds(at * query_block // CORES, query_block // CORES)
            kept = jnp.where(first, tokens[:, 0], tokens[:, 1]).reshape(-1, HEAD_SIZE)
            sent = jnp.where(first, tokens[:, 1], tokens[:, 0]).reshape(-1, HEAD_SIZE)
            numer_refs[0][half, out_columns] = kept
            numer_refs[1][half, out_columns] = sent.astype(jnp.bfloat16)


def attend(whole, keys, values, block_mask, rows_each):
    qtok, width = whole.shape
    kdev = keys.shape[0]
    heads_kv, query_blocks, key_blocks = block_mask.shape
    columns = width // heads_kv
    lanes = columns // HEAD_SIZE * (qtok // query_blocks)
    stat = jax.ShapeDtypeStruct((heads_kv, query_blocks, lanes), jnp.float32)
    stat_spec = pl.BlockSpec((1, query_blocks, lanes), lambda h: (h, 0, 0))
    numers = [jax.ShapeDtypeStruct((qtok, width), jnp.float32)]
    if rows_each:
        numers = [jax.ShapeDtypeStruct((qtok // CORES, width), t) for t in (jnp.float32, jnp.bfloat16)]
    return pl.pallas_call(
        functools.partial(attend_kernel, rows_each),
        grid=(heads_kv,),
        out_shape=(*numers, stat, stat),
        in_specs=[
            pl.BlockSpec(memory_space=pltpu.SMEM),
            pl.BlockSpec((qtok, columns), lambda h: (0, h)),
            pl.BlockSpec((kdev, HEAD_SIZE), lambda h: (0, h)),
            pl.BlockSpec((kdev, HEAD_SIZE), lambda h: (0, h)),
        ],
        out_specs=(
            *(pl.BlockSpec((numer.shape[0], columns), lambda h: (0, h)) for numer in numers),
            stat_spec,
            stat_spec,
        ),
        scratch_shapes=[
            pltpu.SMEM((key_blocks + 2,), jnp.int32),
            pltpu.VMEM(((key_blocks + 1) // 2, 2 * kdev // key_blocks, lanes), jnp.float32),
            pltpu.VMEM((HEAD_SIZE, lanes), jnp.bfloat16),
            pltpu.VMEM((HEAD_SIZE + ONES, kdev), jnp.bfloat16),
            pltpu.VMEM((HEAD_SIZE + ONES, lanes), jnp.float32),
        ],
        compiler_params=pltpu.CompilerParams(vmem_limit_bytes=60 * 2**20),
        name="attend",
    )(block_mask, whole, keys, values)


def by_token(stat, qtok):
    heads_kv, query_blocks, _ = stat.shape
    stat = stat.reshape(heads_kv, query_blocks, -1, qtok // query_blocks)
    return stat.transpose(1, 3, 0, 2).reshape(qtok, -1)


def shards_any(queries, keys, values, block_mask, out_weight):
    whole = lax.all_gather(queries, "ctx", axis=0, tiled=True)
    qtok, width = whole.shape
    numer, top, total = attend(whole, keys, values, block_mask, 0)
    rescale = by_token(jnp.exp2(top - lax.pmax(top, "ctx")), qtok)
    denom = by_token(total, qtok) * rescale
    numer = (numer.reshape(qtok, -1, HEAD_SIZE) * rescale[:, :, None]).reshape(qtok, width)
    num_rows = lax.psum_scatter(numer, "ctx", scatter_dimension=0, tiled=True)
    den_rows = lax.psum_scatter(denom, "ctx", scatter_dimension=0, tiled=True)
    own_rows = num_rows.shape[0]
    attn_rows = (num_rows.reshape(own_rows, -1, HEAD_SIZE) / den_rows[:, :, None]).reshape(
        own_rows, width
    )
    attn_cols = lax.all_to_all(
        attn_rows.astype(jnp.bfloat16), "ctx", split_axis=1, concat_axis=0, tiled=True
    )
    summed = lax.psum_scatter(
        jnp.dot(attn_cols, out_weight, preferred_element_type=jnp.float32),
        "ctx",
        scatter_dimension=0,
        tiled=True,
    )
    return summed.astype(jnp.bfloat16)


def place(n):
    me = lax.axis_index("ctx")
    core = lax.rem(me, CORES)
    x = lax.rem(me // CORES, ROW)
    plane = me // (CORES * ROW)
    return me, plane, x, core


def index_of(plane, x, core):
    return (plane * ROW + x) * CORES + core


def greet(devices):
    barrier = pltpu.get_barrier_semaphore()
    for device in devices:
        pl.semaphore_signal(barrier, inc=1, device_id={"ctx": device}, device_id_type=MESH)
    pl.semaphore_wait(barrier, len(devices))


def remote(src, dst, send, recv, device):
    return pltpu.make_async_remote_copy(
        src_ref=src,
        dst_ref=dst,
        send_sem=send,
        recv_sem=recv,
        device_id={"ctx": device},
        device_id_type=MESH,
    )


def gather_kernel(n, own_ref, whole_ref, own_sem, send_sem, recv_sem):
    me, plane, x, core = place(n)
    planes = n // (CORES * ROW)
    beside, sibling = 1 - x, 1 - core
    barrier = pltpu.get_barrier_semaphore()

    def hello(device):
        pl.semaphore_signal(barrier, inc=1, device_id={"ctx": device}, device_id_type=MESH)

    hello(index_of(plane, beside, core))
    hello(index_of(plane, x, sibling))

    @pl.when(plane > 0)
    def _():
        hello(index_of(plane - 1, x, core))

    @pl.when(plane < planes - 1)
    def _():
        hello(index_of(plane + 1, x, core))

    ends = (plane > 0).astype(jnp.int32) + (plane < planes - 1).astype(jnp.int32)
    pl.semaphore_wait(barrier, 2 + ends)
    own = pltpu.make_async_copy(own_ref, whole_ref.at[me], own_sem)
    own.start()

    def copy_to(block, way, device, mine=False):
        src = own_ref if mine else whole_ref.at[block]
        return remote(src, whole_ref.at[block], send_sem.at[way, block], recv_sem.at[block], device)

    def arrived(block):
        copy_to(block, 0, me).wait_recv()

    def pass_on(p, up, act, mine=False):
        block = index_of(p, x, core)

        @pl.when(plane + up < planes if up > 0 else plane + up >= 0)
        def _():
            act(copy_to(block, 0 if up > 0 else 1, index_of(plane + up, x, core), mine))

    start, ended = (lambda copy: copy.start()), (lambda copy: copy.wait_send())
    pass_on(plane, 1, start, True)
    pass_on(plane, -1, start, True)
    copy_to(me, 2, index_of(plane, beside, core), True).start()
    copy_to(me, 3, index_of(plane, x, sibling), True).start()
    for distance in range(1, planes):
        for up in (1, -1):
            p = plane - up * distance

            @pl.when(p >= 0 if up > 0 else p < planes)
            def _():
                block = index_of(p, x, core)
                arrived(block)
                pass_on(p, up, start)
                copy_to(block, 2, index_of(plane, beside, core)).start()
                copy_to(block, 3, index_of(plane, x, sibling)).start()

    def near_first(act):
        act(plane)
        for distance in range(1, planes):
            for up in (1, -1):
                p = plane - up * distance

                @pl.when(p >= 0 if up > 0 else p < planes)
                def _():
                    act(p)

    def from_beside(p):
        block = index_of(p, beside, core)
        arrived(block)
        copy_to(block, 3, index_of(plane, x, sibling)).start()

    def from_sibling(p):
        arrived(index_of(p, x, sibling))
        arrived(index_of(p, beside, sibling))

    near_first(from_beside)
    near_first(from_sibling)
    pass_on(plane, 1, ended, True)
    pass_on(plane, -1, ended, True)
    for distance in range(1, planes):
        for up in (1, -1):
            p = plane - up * distance

            @pl.when(p >= 0 if up > 0 else p < planes)
            def _():
                pass_on(p, up, ended)

    def sent(p):
        copy_to(index_of(p, x, core), 2, index_of(plane, beside, core)).wait_send()
        copy_to(index_of(p, x, core), 3, index_of(plane, x, sibling)).wait_send()
        copy_to(index_of(p, beside, core), 3, index_of(plane, x, sibling)).wait_send()

    near_first(sent)
    own.wait()


def gather_rows(queries, n):
    rows, width = queries.shape
    whole = pl.pallas_call(
        functools.partial(gather_kernel, n),
        out_shape=jax.ShapeDtypeStruct((n, rows, width), queries.dtype),
        in_specs=[pl.BlockSpec(memory_space=pltpu.VMEM)],
        out_specs=pl.BlockSpec(memory_space=pltpu.VMEM),
        scratch_shapes=[
            pltpu.SemaphoreType.DMA,
            pltpu.SemaphoreType.DMA((4, n)),
            pltpu.SemaphoreType.DMA((n,)),
        ],
        compiler_params=pltpu.CompilerParams(collective_id=0, has_side_effects=True),
        name="gather_rows",
    )(queries)
    return whole.reshape(n * rows, width)


def reduce_rows(place_of, parts, merge, finish):
    plane, x, core, planes = place_of
    beside, sibling = 1 - x, 1 - core
    others = [lax.rem(plane + step, planes) for step in range(1, planes)]

    def turn(step):
        return lax.rem(plane + 1 + step, planes)

    def core_copy(part, p):
        sem = part[9]
        return remote(
            part[0](p), part[2].at[p], sem.at[0, p], sem.at[1, p], index_of(plane, x, sibling)
        )

    def beside_copy(part, p):
        sem = part[9]
        return remote(
            part[3].at[p], part[5].at[p], sem.at[2, p], sem.at[3, p], index_of(plane, beside, core)
        )

    def plane_copy(part, p, slot):
        sem = part[9]
        return remote(
            part[6].at[p], part[8].at[slot], sem.at[4, p], sem.at[5, slot], index_of(p, x, core)
        )

    for p in others + [plane]:
        for part in parts:
            core_copy(part, p).start()

    def from_core(step, _):
        p = turn(step)
        for part in parts:
            core_copy(part, p).wait_recv()
        for side, out in ((beside, 3), (x, 4)):
            merge(
                [part[1](p, side) for part in parts],
                [part[2].at[p, side] for part in parts],
                [part[out].at[p] for part in parts],
            )
            if out == 3:
                for part in parts:
                    beside_copy(part, p).start()
        return 0

    lax.fori_loop(0, planes, from_core, 0)

    def from_beside(p, outs):
        for part in parts:
            beside_copy(part, p).wait_recv()
        merge([part[4].at[p] for part in parts], [part[5].at[p] for part in parts], outs)

    def to_plane(step, _):
        p = turn(step)
        from_beside(p, [part[6].at[p] for part in parts])
        for part in parts:
            plane_copy(part, p, plane).start()
        return 0

    lax.fori_loop(0, planes - 1, to_plane, 0)
    from_beside(plane, [part[7] for part in parts])
    for p in others:
        for part in parts:
            plane_copy(part, p, p).wait_recv()
    finish([[part[7] for part in parts]] + [[part[8].at[p] for part in parts] for p in others])
    for p in others + [plane]:
        for part in parts:
            core_copy(part, p).wait_send()
            beside_copy(part, p).wait_send()
    for p in others:
        for part in parts:
            plane_copy(part, p, plane).wait_send()


def reduce_scratch(planes, rows, width, dtype):
    return [
        pltpu.VMEM((planes, ROW, rows, width), dtype),
        pltpu.VMEM((planes, rows, width), dtype),
        pltpu.VMEM((planes, rows, width), jnp.float32),
        pltpu.VMEM((planes, rows, width), dtype),
        pltpu.VMEM((planes, rows, width), dtype),
        pltpu.VMEM((rows, width), jnp.float32),
        pltpu.VMEM((planes, rows, width), dtype),
        pltpu.SemaphoreType.DMA((6, planes)),
    ]


STATS = 128


def weigh(stats):
    half = STATS // 2
    tops = [stat[:, :half] for stat in stats]
    top = functools.reduce(jnp.maximum, tops)
    factors = [jnp.exp2(one - top) for one in tops]
    total = sum(stat[:, half:] * factor for stat, factor in zip(stats, factors))
    return top, factors, total


def combine_kernel(n, kept_hbm, sent_ref, stat_ref, cols_ref, *scratch):
    numer_scratch, stat_scratch = scratch[:8], scratch[8:16]
    piece_ref, swap_send, swap_recv, own_sem, kept_ref, kept_sem = scratch[16:]
    keep = pltpu.make_async_copy(kept_hbm, kept_ref, kept_sem)
    keep.start()
    me, plane, x, core = place(n)
    planes = n // (CORES * ROW)
    width = kept_ref.shape[-1]
    heads = width // HEAD_SIZE
    others = [lax.rem(me + step, n) for step in range(1, n)]
    greet(others)
    keep.wait()

    def merge(one, two, out):
        top, factors, total = weigh([one[1][...], two[1][...]])
        out[1][...] = jnp.concatenate([top, total], axis=1)
        for head in range(heads):
            at = slice(head * HEAD_SIZE, (head + 1) * HEAD_SIZE)
            out[0][:, at] = (
                one[0][:, at].astype(jnp.float32) * factors[0][:, head : head + 1]
                + two[0][:, at].astype(jnp.float32) * factors[1][:, head : head + 1]
            ).astype(out[0].dtype)

    def finish(sources):
        _, factors, total = weigh([source[1][...] for source in sources])
        out = []
        for head in range(heads):
            at = slice(head * HEAD_SIZE, (head + 1) * HEAD_SIZE)
            numer = sum(
                source[0][:, at].astype(jnp.float32) * factor[:, head : head + 1]
                for source, factor in zip(sources, factors)
            )
            out.append((numer / total[:, head : head + 1]).astype(jnp.bfloat16))
        attn = jnp.concatenate(out, axis=1)
        share = width // n
        for device in range(n):
            piece_ref[device] = attn[:, device * share : (device + 1) * share]

    reduce_rows(
        (plane, x, core, planes),
        [
            (lambda p: sent_ref.at[p], lambda p, side: kept_ref.at[p, side], *numer_scratch),
            (
                lambda p: stat_ref.at[p, :, 1 - core],
                lambda p, side: stat_ref.at[p, side, core],
                *stat_scratch,
            ),
        ],
        merge,
        finish,
    )

    def swap(device, slot):
        return remote(
            piece_ref.at[device], cols_ref.at[slot], swap_send.at[device], swap_recv.at[slot], device
        )

    own = pltpu.make_async_copy(piece_ref.at[me], cols_ref.at[me], own_sem)
    own.start()
    for device in others:
        swap(device, me).start()
    own.wait()
    for device in others:
        swap(device, device).wait_recv()
    for device in others:
        swap(device, me).wait_send()


def combine(kept, sent, stats, n):
    qtok, width = stats.shape[0], kept.shape[1]
    planes, rows = n // (CORES * ROW), qtok // n
    cols = pl.pallas_call(
        functools.partial(combine_kernel, n),
        out_shape=jax.ShapeDtypeStruct((n, rows, width // n), jnp.bfloat16),
        in_specs=[pl.BlockSpec(memory_space=pl.ANY)] * 2
        + [pl.BlockSpec(memory_space=pltpu.VMEM)],
        out_specs=pl.BlockSpec(memory_space=pltpu.VMEM),
        scratch_shapes=reduce_scratch(planes, rows, width, jnp.bfloat16)
        + reduce_scratch(planes, rows, STATS, jnp.float32)
        + [
            pltpu.VMEM((n, rows, width // n), jnp.bfloat16),
            pltpu.SemaphoreType.DMA((n,)),
            pltpu.SemaphoreType.DMA((n,)),
            pltpu.SemaphoreType.DMA,
            pltpu.VMEM((planes, ROW, rows, width), jnp.float32),
            pltpu.SemaphoreType.DMA,
        ],
        compiler_params=pltpu.CompilerParams(
            collective_id=1, has_side_effects=True, vmem_limit_bytes=60 * 2**20
        ),
        name="combine",
    )(
        kept.reshape(planes, ROW, rows, width),
        sent.reshape(planes, ROW, rows, width),
        stats.reshape(planes, ROW, CORES, rows, STATS),
    )
    return cols.reshape(qtok, width // n)


TILE = 1024


def project_kernel(n, cols_ref, weight_hbm, out_ref, weight_ref, weight_sem, kept_ref, sent_ref, *scratch):
    _, plane, x, core = place(n)
    planes = n // (CORES * ROW)
    rows, width = out_ref.shape

    def fetch(tile):
        at = pl.ds(pl.multiple_of(tile * TILE, TILE), TILE)
        return pltpu.make_async_copy(weight_hbm.at[:, at], weight_ref.at[:, at], weight_sem.at[tile])

    for tile in range(width // TILE):
        fetch(tile).start()
    greet(
        [index_of(lax.rem(plane + step, planes), x, core) for step in range(1, planes)]
        + [index_of(plane, 1 - x, core), index_of(plane, x, 1 - core)]
    )

    def tile_step(tile, _):
        at = pl.ds(pl.multiple_of(tile * TILE, TILE), TILE)
        fetch(tile).wait()
        product = jnp.dot(cols_ref[...], weight_ref[:, at], preferred_element_type=jnp.float32)
        product = product.reshape(planes, ROW, CORES, rows, TILE)
        kept_ref[:, :, :, at] = jnp.where(core == 0, product[:, :, 0], product[:, :, 1])
        sent = jnp.where(core == 0, product[:, :, 1], product[:, :, 0])
        sent_ref[:, :, :, at] = sent.astype(sent_ref.dtype)
        return 0

    lax.fori_loop(0, width // TILE, tile_step, 0)

    def merge(one, two, out):
        out[0][...] = (one[0][...].astype(jnp.float32) + two[0][...].astype(jnp.float32)).astype(
            out[0].dtype
        )

    def finish(sources):
        out_ref[...] = sum(source[0][...].astype(jnp.float32) for source in sources).astype(
            out_ref.dtype
        )

    reduce_rows((plane, x, core, planes), [(lambda p: sent_ref.at[p], lambda p, side: kept_ref.at[p, side], *scratch)], merge, finish)


def project(cols, weight, n):
    qtok = cols.shape[0]
    width = weight.shape[1]
    planes, rows = n // (CORES * ROW), qtok // n
    return pl.pallas_call(
        functools.partial(project_kernel, n),
        out_shape=jax.ShapeDtypeStruct((rows, width), jnp.bfloat16),
        in_specs=[pl.BlockSpec(memory_space=pltpu.VMEM), pl.BlockSpec(memory_space=pl.ANY)],
        out_specs=pl.BlockSpec(memory_space=pltpu.VMEM),
        scratch_shapes=[
            pltpu.VMEM(weight.shape, weight.dtype),
            pltpu.SemaphoreType.DMA((width // TILE,)),
        ]
        + [pltpu.VMEM((planes, ROW, rows, width), t) for t in (jnp.float32, jnp.bfloat16)]
        + reduce_scratch(planes, rows, width, jnp.bfloat16),
        compiler_params=pltpu.CompilerParams(
            collective_id=2, has_side_effects=True, vmem_limit_bytes=60 * 2**20
        ),
        name="project",
    )(cols, weight)


def shards_near(n, queries, keys, values, block_mask, out_weight):
    whole = gather_rows(queries, n)
    qtok = whole.shape[0]
    kept, sent, top, total = attend(whole, keys, values, block_mask, queries.shape[0])
    top, total = by_token(top, qtok), by_token(total, qtok)
    room = ((0, 0), (0, STATS // 2 - top.shape[1]))
    stats = jnp.concatenate([jnp.pad(top, room), jnp.pad(total, room)], axis=1)
    cols = combine(kept, sent, stats, n)
    return project(cols, out_weight, n)


def solution(mesh):
    n = mesh.shape["ctx"]

    def shards(queries, *rest):
        fits = n % (CORES * ROW) == 0 and queries.shape[0] == 16
        if fits and queries.shape[1] // HEAD_SIZE <= STATS // 2:
            return shards_near(n, queries, *rest)
        return shards_any(queries, *rest)

    return jax.shard_map(
        shards,
        mesh=mesh,
        in_specs=(
            P(("groups", "ctx"), None),
            P(("groups", "ctx"), None),
            P(("groups", "ctx"), None),
            P("groups", None, "ctx"),
            P("ctx", None),
        ),
        out_specs=P(("groups", "ctx"), None),
        check_vma=False,
    )
```
